256 devices in a mesh: orb: 64 (over x, z, core), wall: 4 (over y).
Axes of the slice: x: 4, y: 4, z: 8, core: 2. Of those that a mesh axis runs over, the one named last changes fastest.
Arguments:
- fluid_state: float32 [8, 786432], P(None, ('orb', 'wall')), may hold values from -4 to 4, as said below
- ghost_list: int32 [7, 1536], P(None, ('orb', 'wall')), may hold values from 0 to 23, as said below
- pair_list: int32 [6144, 14], P(('orb', 'wall')), may hold values from 0 to 65, as said below
- wall_state: float32 [4, 196608], P(None, ('orb', 'wall')), may hold values from 0 to 0.6, as said below
- wall_count: int32 [1536], P(('orb', 'wall')), may hold values from 1 to 128, as said below
- wall_pairs: int32 [6144, 4], P(('orb', 'wall')), may hold values from 0 to 7, as said below
Outputs:
- density_rate: float32 [786432], P(('orb', 'wall'))
- acceleration: float32 [3, 786432], P(None, ('orb', 'wall'))
- time_step: float32 [], replicated
The draws below stay inside these ranges and needn't reach their ends.
Inputs may be any that keep to these rules, and one draw needn't show every extreme that they name: `fluid_state`: rows: position from 0 to 0.6, velocity from -4 to 4, density from 0.97 to 1.03, mass from 0.001 to 0.003. `ghost_list`: the 6 entries of one mask and one domain are distinct. `pair_list`: the 14 entries of one block are distinct, and every candidate index is named by some block of each domain. `wall_state`: rows: x and y from 0 to 0.6, z from 0 to 0.15, mass from 0.001 to 0.003. `wall_count`: the live particles fill the first columns of their wall block. `wall_pairs`: the 4 entries of one block are distinct, and every wall candidate index is named by some block of each domain.
All inputs are finite; a program needn't handle non-finite values.
Results may differ from the reference program's by a relative error of at most 0.0003.
Values sent between devices are 32-bit elements; how exact they have to be, the bound alone decides.
A program may use at most 64 MiB of HBM per device.

```python
import jax
import jax.numpy as jnp
from jax import lax

NB = 24
K = 14
KW = 4
GH = 6
WB = 6
EB = 1
DOMAINS = 256
PARTICLES = 786432
WALLS = 196608
N_ORB = 64
N_WALL = 4


def draw_fluid_state(key, part):
    keys = jax.random.split(key, 5)
    position = jax.random.uniform(keys[0], (3, PARTICLES), jnp.float32, 0.0, 0.6)
    velocity = jnp.clip(jax.random.normal(keys[2], (3, PARTICLES), jnp.float32), -4.0, 4.0)
    density = jax.random.uniform(keys[3], (1, PARTICLES), jnp.float32, 0.97, 1.03)
    masses = jax.random.uniform(keys[4], (1, PARTICLES), jnp.float32, 0.001, 0.003)
    return jnp.concatenate([position, velocity, density, masses], axis=0).astype(jnp.float32)


def draw_wall_state(key, part):
    keys = jax.random.split(key, 3)
    plane = jax.random.uniform(keys[0], (2, WALLS), jnp.float32, 0.0, 0.6)
    height = jax.random.uniform(keys[1], (1, WALLS), jnp.float32, 0.0, 0.15)
    masses = jax.random.uniform(keys[2], (1, WALLS), jnp.float32, 0.001, 0.003)
    return jnp.concatenate([plane, height, masses], axis=0).astype(jnp.float32)


def draw_ghost_list(key, part):
    keys = jax.random.split(key, 7 * DOMAINS)

    def pick_rows(single):
        return jax.random.permutation(single, NB)[:GH]
    rows = jax.vmap(pick_rows)(keys)
    return rows.reshape(7, DOMAINS * GH).astype(jnp.int32)


def spread_lists(key, blocks_per, listed, choices_total):
    keys = jax.random.split(key, DOMAINS)
    picks = (jnp.arange(blocks_per)[:, None] * listed + jnp.arange(listed)[None, :]) % choices_total

    def pick_rows(single):
        return jax.random.permutation(single, choices_total)[picks]
    rows = jax.vmap(pick_rows)(keys)
    return rows.reshape(DOMAINS * blocks_per, listed).astype(jnp.int32)


def draw_pair_list(key, part):
    return spread_lists(jax.random.fold_in(key, 11), NB, K, NB + 7 * GH)


def draw_wall_pairs(key, part):
    return spread_lists(jax.random.fold_in(key, 23), NB, KW, WB + 2 * EB)


def draw_wall_count(key, part):
    keys = jax.random.split(key, 3)
    pillar = jax.random.randint(keys[0], (DOMAINS * WB,), 0, 4) == 0
    sparse = jax.random.randint(keys[1], (DOMAINS * WB,), 1, 65)
    counts = jnp.where(pillar, 128, sparse)
    forced = jax.random.randint(keys[2], (), 0, DOMAINS * WB)
    return counts.at[forced].set(128).astype(jnp.int32)


def setup_inputs(seed: int = 0) -> dict:
    key_of = jax.random.split(jax.random.key(seed), 7)
    fluid_state = draw_fluid_state(jax.random.fold_in(key_of[6], 71), 0)
    ghost_list = draw_ghost_list(jax.random.fold_in(key_of[6], 71), 0)
    pair_list = draw_pair_list(jax.random.fold_in(key_of[6], 71), 0)
    wall_state = draw_wall_state(jax.random.fold_in(key_of[6], 71), 0)
    wall_count = draw_wall_count(jax.random.fold_in(key_of[6], 71), 0)
    wall_pairs = draw_wall_pairs(jax.random.fold_in(key_of[6], 71), 0)
    return {"fluid_state": fluid_state, "ghost_list": ghost_list, "pair_list": pair_list, "wall_state": wall_state, "wall_count": wall_count, "wall_pairs": wall_pairs}


smoothing = 0.1
support = 0.3
kernel_norm = 21.0 / (2.0 * 3.141592653589793 * support ** 3)
grad_coeff = -20.0 / support ** 2 * kernel_norm
tait_coeff = 25.0 / 7.0
visc_coeff = 0.05
cohesion = 2000.0
adhesion = 2000.0
gravity = 9.81
courant = 0.25

def kernel_parts(target_pos, source_pos):
    offset = target_pos[None, :, :, None] - source_pos[:, :, None, :]
    dist_sq = lax.optimization_barrier(jnp.sum(offset * offset, axis=1))
    radius = jnp.sqrt(dist_sq)
    scaled = radius / support
    falloff = jnp.maximum(1.0 - scaled, 0.0)
    cubed = falloff * falloff * falloff
    return (offset, dist_sq, grad_coeff * cubed, cubed * (4.0 * scaled - 1.0))

def pressure_of(density):
    return tait_coeff * (density ** 7 - 1.0)

def block_terms(target, sources, walls):
    target_pos = target[0:3]
    target_vel = target[3:6]
    target_rho = target[6]
    target_press = pressure_of(target_rho)
    source_rho = sources[:, 6]
    offset, dist_sq, grad_scale, pull = kernel_parts(target_pos, sources[:, 0:3])
    vel_diff = target_vel[None, :, :, None] - sources[:, 3:6][:, :, None, :]
    approach = lax.optimization_barrier(jnp.sum(vel_diff * offset, axis=1))
    mass_row = sources[:, 7][:, None, :]
    fluid_rate = lax.optimization_barrier(jnp.sum(mass_row * approach * grad_scale, axis=(0, 2)))
    mean_rho = 0.5 * (target_rho[None, :, None] + source_rho[:, None, :])
    viscous = -visc_coeff * jnp.minimum(approach, 0.0) / ((dist_sq + 0.0001) * mean_rho)
    press_term = (target_press / target_rho ** 2)[None, :, None] + (pressure_of(source_rho) / source_rho ** 2)[:, None, :] + viscous
    weight = mass_row * (press_term * grad_scale + cohesion * pull)
    fluid_force = -lax.optimization_barrier(jnp.sum(weight[:, None] * offset, axis=(0, 3)))
    wall_offset, wall_dist, wall_grad, wall_pull = kernel_parts(target_pos, walls[:, 0:3])
    wall_masses = walls[:, 3][:, None, :]
    wall_approach = lax.optimization_barrier(jnp.sum(target_vel[None, :, :, None] * wall_offset, axis=1))
    wall_rate = lax.optimization_barrier(jnp.sum(wall_masses * wall_approach * wall_grad, axis=(0, 2)))
    own_press = (2.0 * target_press / target_rho ** 2)[None, :, None]
    wall_weight = wall_masses * (own_press * wall_grad + adhesion * wall_pull)
    wall_force = -lax.optimization_barrier(jnp.sum(wall_weight[:, None] * wall_offset, axis=(0, 3)))
    downward = jnp.array([0.0, 0.0, -gravity], jnp.float32)[:, None]
    return (fluid_rate + wall_rate, fluid_force + wall_force + downward)

def reference(fluid_state, ghost_list, pair_list, wall_state, wall_count, wall_pairs):
    domains = N_ORB * N_WALL
    blocks = jnp.transpose(fluid_state.reshape(8, domains * NB, 128), (1, 0, 2))
    ghost_table = ghost_list.reshape(7, domains, GH)
    alive = (jnp.arange(128, dtype=jnp.int32)[None, :] < wall_count[:, None]).astype(jnp.float32).reshape(-1)
    wall_live = jnp.concatenate([wall_state[0:3], wall_state[3:4] * alive[None, :]], axis=0)
    wall_blocks = jnp.transpose(wall_live.reshape(4, domains * WB, 128), (1, 0, 2))
    pair_table = pair_list.reshape(domains, NB, K)
    wall_table = wall_pairs.reshape(domains, NB, KW)
    patterns = jnp.arange(1, 8, dtype=jnp.int32)
    local_ids = jnp.arange(NB, dtype=jnp.int32)
    edge_ids = jnp.arange(EB, dtype=jnp.int32)

    def one_domain(domain):
        orb_place = domain // N_WALL
        wall_place = domain % N_WALL
        partners = jnp.bitwise_xor(orb_place, patterns) * N_WALL + wall_place
        chosen = ghost_table[patterns - 1, partners]
        ghost_ids = (partners[:, None] * NB + chosen).reshape(-1)
        candidates = blocks[jnp.concatenate([domain * NB + local_ids, ghost_ids])]
        below = wall_blocks[jnp.maximum(domain - 1, 0) * WB + WB - EB + edge_ids]
        below = jnp.where(wall_place > 0, below, jnp.zeros_like(below))
        above = wall_blocks[jnp.minimum(domain + 1, domains - 1) * WB + edge_ids]
        above = jnp.where(wall_place < N_WALL - 1, above, jnp.zeros_like(above))
        own_walls = wall_blocks[domain * WB + jnp.arange(WB, dtype=jnp.int32)]
        wall_cands = jnp.concatenate([below, own_walls, above], axis=0)

        def per_block(inputs):
            return block_terms(inputs[0], candidates[inputs[1]], wall_cands[inputs[2]])
        return lax.map(per_block, (candidates[0:NB], pair_table[domain], wall_table[domain]))
    rates, forces = lax.map(one_domain, jnp.arange(domains, dtype=jnp.int32))
    density_rate = rates.reshape(-1)
    acceleration = jnp.transpose(forces, (2, 0, 1, 3)).reshape(3, -1)
    peak = jnp.max(jnp.sqrt(lax.optimization_barrier(jnp.sum(acceleration * acceleration, axis=0))))
    time_step = courant * jnp.sqrt(smoothing / (peak + 1e-06))
    return (density_rate, acceleration, time_step)
```

```python
import jax
import jax.numpy as jnp
from jax import lax
from jax.experimental import pallas as pl
from jax.experimental.pallas import tpu as pltpu
from jax.sharding import PartitionSpec as P

NB = 24
K = 14
KW = 4
GH = 6
WB = 6
EB = 1
NC = NB + 7 * GH
NW = WB + 2 * EB
LN = 128

smoothing = 0.1
support = 0.3
kernel_norm = 21.0 / (2.0 * 3.141592653589793 * support**3)
grad_coeff = -20.0 / support**2 * kernel_norm
tait_coeff = 25.0 / 7.0
visc_coeff = 0.05
cohesion = 2000.0
adhesion = 2000.0
gravity = 9.81
courant = 0.25

center = 0.3
inv_support = 1.0 / support
eps_scaled = 0.0001 / support**2
visc_scaled = visc_coeff * -grad_coeff / support

F32 = jnp.float32
BF16 = jnp.bfloat16


def split(value, terms):
    parts = []
    for _ in range(terms - 1):
        high = value.astype(BF16).astype(F32)
        parts.append(high)
        value = value - high
    parts.append(value.astype(BF16).astype(F32))
    return parts


def pressure_of(density):
    return tait_coeff * (density**7 - 1.0)


def dot3(a, b):
    return a[0] * b[0] + a[1] * b[1] + a[2] * b[2]


CROSS = ((0, 0), (0, 1), (0, 2), (1, 0), (1, 1), (2, 0))


def source_rows(y, v, rho_half):
    ys = [split(c, 3) for c in y]
    norm = split(dot3(y, y), 3)
    one = jnp.ones_like(y[0])
    rows = []
    for c in range(3):
        rows += [ys[c][j] for j, _ in CROSS]
    rows += [one] * 3
    rows += norm
    if v is None:
        return rows
    vs = [split(c, 2) for c in v]
    vt = [c[0] + c[1] for c in vs]
    for c in range(3):
        rows += [vs[c][0], vs[c][0], vs[c][0], vs[c][1], vs[c][1]]
    rows += split(dot3(vt, y), 3)
    rows += [norm[0], norm[0], norm[1]]
    rows += split(rho_half * dot3(y, y), 3)
    hs = split(rho_half, 3)
    rows += [hs[j] for j, _ in CROSS]
    for c in range(3):
        hy = split(rho_half * y[c], 3)
        rows += [hy[j] for j, _ in CROSS]
    return rows


def target_rows(y, v, rho_half):
    ys = [split(c, 3) for c in y]
    vs = [split(c, 2) for c in v]
    vt = [c[0] + c[1] for c in vs]
    sq = dot3(y, y)
    norm = split(sq, 3)
    reach = sq + eps_scaled
    vy = split(dot3(vt, y), 3)
    hs = split(rho_half, 3)
    hn = split(rho_half * reach, 3)
    rs = split(reach, 3)
    one = jnp.ones_like(y[0])
    zero = jnp.zeros_like(y[0])
    rows = []
    for c in range(3):
        hy = split(rho_half * y[c], 3)
        for _, i in CROSS:
            approach = -vs[c][i] if i < 2 else zero
            rows.append((-2.0 * ys[c][i], approach, -2.0 * hy[i]))
    for i in range(3):
        rows.append((norm[i], vy[i], hn[i]))
    for i in range(3):
        rows.append((one, zero, hs[0]))
    for c in range(3):
        for i in (0, 1, 2, 0, 1):
            rows.append((zero, -ys[c][i], zero))
    rows += [(zero, one, zero)] * 3
    rows += [(zero, zero, hs[1]), (zero, zero, hs[2]), (zero, zero, hs[1])]
    rows += [(zero, zero, one)] * 3
    for _, i in CROSS:
        rows.append((zero, zero, rs[i]))
    for c in range(3):
        for _, i in CROSS:
            rows.append((zero, zero, -2.0 * ys[c][i]))
    return rows


KR = 72
KWALL = 24


def column_rows(quantities):
    parts = [split(q, 2) for q in quantities]
    return [p[0] for p in parts], [p[1] for p in parts]


def falloff_of(dist_sq):
    dist_sq = jnp.maximum(dist_sq, 1e-30)
    s = jnp.maximum(1.0 - dist_sq * lax.rsqrt(dist_sq), 0.0)
    return s, s * s * s


def two_terms(value):
    high = value.astype(BF16)
    return high, (value - high.astype(F32)).astype(BF16)


def pair_kernel(
    pair_ref, wpair_ref, own_ref, ghost_ref, wall_ref, rate_ref, accel_ref, peak_ref,
    cand, wcand, jf32, if32, wf32, cl32, wc32, jf, tf, wf, cl, wc, sums, wsums,
):
    for b in range(NB):
        cand[8 * b : 8 * b + 8, :] = own_ref[:, LN * b : LN * b + LN]
    cand[8 * NB :, :] = ghost_ref[...]
    for b in range(NW):
        wcand[4 * b : 4 * b + 4, :] = wall_ref[:, LN * b : LN * b + LN]

    state = [cand[pl.ds(r, NC, stride=8), :] for r in range(8)]
    y = [(state[c] - center) * inv_support for c in range(3)]
    v = state[3:6]
    rho, mass = state[6], state[7]
    rho_half = (0.5 / visc_scaled) * rho
    push = pressure_of(rho) / (rho * rho)

    rows = source_rows(y, v, rho_half)
    assert len(rows) == KR
    for k, row in enumerate(rows):
        jf32[pl.ds(k, NC, stride=KR), :] = row
    vt = v
    cols = [mass] + [mass * c for c in y] + [mass * c for c in vt]
    cols += [mass * dot3(vt, y), mass * push] + [mass * push * c for c in y]
    high, low = column_rows(cols)
    cl32[...] = jnp.zeros_like(cl32)
    for k in range(12):
        cl32[pl.ds(k, NC, stride=32), :] = high[k]
        cl32[pl.ds(16 + k, NC, stride=32), :] = low[k]

    ty = [c[:NB] for c in y]
    tv = [c[:NB] for c in v]
    weights = target_rows(ty, tv, rho_half[:NB])
    assert len(weights) == KR
    for k, row in enumerate(weights):
        for part in range(3):
            if32[part, pl.ds(k, NB, stride=KR), :] = row[part]

    wstate = [wcand[pl.ds(r, NW, stride=4), :] for r in range(4)]
    wy = [(wstate[c] - center) * inv_support for c in range(3)]
    wrows = source_rows(wy, None, None)
    assert len(wrows) == KWALL
    for k, row in enumerate(wrows):
        wf32[pl.ds(k, NW, stride=KWALL), :] = row
    whigh, wlow = column_rows([wstate[3]] + [wstate[3] * c for c in wy])
    wc32[...] = jnp.zeros_like(wc32)
    for k in range(4):
        wc32[pl.ds(k, NW, stride=16), :] = whigh[k]
        wc32[pl.ds(8 + k, NW, stride=16), :] = wlow[k]

    def build_source(b, carry):
        rows = jf32[pl.ds(b * KR, KR), :]
        rows = jnp.concatenate([rows, jnp.zeros((LN - KR, LN), F32)], axis=0)
        jf[b] = rows.T.astype(BF16)
        c = cl32[pl.ds(b * 32, 32), :].astype(BF16)
        cl[b] = jnp.concatenate([c, c], axis=1)
        return carry

    lax.fori_loop(0, NC, build_source, 0, unroll=6)

    def build_target(b, carry):
        for part in range(3):
            rows = if32[part, pl.ds(b * KR, KR), :]
            rows = jnp.concatenate([rows, jnp.zeros((LN - KR, LN), F32)], axis=0)
            tf[b, :, LN * part : LN * part + LN] = rows.astype(BF16)
        return carry

    lax.fori_loop(0, NB, build_target, 0)

    def build_wall(b, carry):
        rows = wf32[pl.ds(b * KWALL, KWALL), :]
        rows = jnp.concatenate([rows, jnp.zeros((LN - KWALL, LN), F32)], axis=0)
        wf[b] = rows.T.astype(BF16)
        c = wc32[pl.ds(b * 16, 16), :].astype(BF16)
        wc[b] = jnp.concatenate([c, c], axis=1)
        return carry

    lax.fori_loop(0, NW, build_wall, 0)

    def block(b, carry):
        weights = tf[b]
        total = jnp.zeros((32, 2 * LN), F32)
        for k in range(K):
            j = pair_ref[b, k]
            geo = jnp.dot(jf[j], weights, preferred_element_type=F32)
            s, cubed = falloff_of(geo[:, :LN])
            root = lax.rsqrt(geo[:, 2 * LN :])
            drag = jnp.minimum(geo[:, LN : 2 * LN], 0.0) * (root * root)
            pull = cubed * (drag + (3.0 * cohesion - 4.0 * cohesion * s))
            sh, sl = two_terms(cubed)
            uh, ul = two_terms(pull)
            mat = jnp.concatenate(
                [jnp.concatenate([sh, uh], axis=1), jnp.concatenate([sl, ul], axis=1)], axis=0
            )
            total += jnp.dot(cl[j], mat, preferred_element_type=F32)
        sums[b] = total[:16] + total[16:]
        wtotal = jnp.zeros((16, 2 * LN), F32)
        for k in range(KW):
            j = wpair_ref[b, k]
            geo = jnp.dot(wf[j], weights[:, :LN], preferred_element_type=F32)
            s, cubed = falloff_of(geo)
            pull = cubed * (3.0 * adhesion - 4.0 * adhesion * s)
            sh, sl = two_terms(cubed)
            uh, ul = two_terms(pull)
            mat = jnp.concatenate(
                [jnp.concatenate([sh, uh], axis=1), jnp.concatenate([sl, ul], axis=1)], axis=0
            )
            wtotal += jnp.dot(wc[j], mat, preferred_element_type=F32)
        wsums[b] = wtotal[:8] + wtotal[8:]
        return carry

    lax.fori_loop(0, NB, block, 0)

    def take(ref, row, lane):
        return ref[:, row, lane : lane + LN]

    spart = [take(sums, r, 0) for r in range(12)]
    upart = [take(sums, r, LN) for r in range(4)]
    wspart = [take(wsums, r, 0) for r in range(4)]
    wupart = [take(wsums, r, LN) for r in range(4)]
    own_push = push[:NB]
    rate = (
        dot3(tv, ty) * (spart[0] + wspart[0])
        - dot3(tv, [spart[1 + c] + wspart[1 + c] for c in range(3)])
        - dot3(spart[4:7], ty)
        + spart[7]
    )
    rate_ref[...] = (grad_coeff * support) * rate
    square = jnp.zeros((NB, LN), F32)
    for c in range(3):
        pressed = own_push * (
            ty[c] * (spart[0] + 2.0 * wspart[0]) - (spart[1 + c] + 2.0 * wspart[1 + c])
        )
        pressed += ty[c] * spart[8] - spart[9 + c]
        pulled = ty[c] * (upart[0] + wupart[0]) - (upart[1 + c] + wupart[1 + c])
        force = (-grad_coeff * support) * pressed - support * pulled
        if c == 2:
            force = force - gravity
        square += force * force
        for b in range(NB):
            accel_ref[c : c + 1, LN * b : LN * b + LN] = force[b : b + 1]
    peak = jnp.max(jnp.sqrt(square), axis=0, keepdims=True)
    peak_ref[...] = jnp.broadcast_to(jnp.max(peak, axis=1, keepdims=True), (8, LN))


def pair_forces(pairs, wpairs, own, ghosts, walls, **kw):
    vmem = pl.BlockSpec(memory_space=pltpu.VMEM)
    smem = pl.BlockSpec(memory_space=pltpu.SMEM)
    return pl.pallas_call(
        pair_kernel,
        name="pair_forces",
        out_shape=(
            jax.ShapeDtypeStruct((NB, LN), F32),
            jax.ShapeDtypeStruct((3, NB * LN), F32),
            jax.ShapeDtypeStruct((8, LN), F32),
        ),
        in_specs=[smem, smem, vmem, vmem, vmem],
        out_specs=(vmem, vmem, vmem),
        scratch_shapes=[
            pltpu.VMEM((NC * 8, LN), F32),
            pltpu.VMEM((NW * 4, LN), F32),
            pltpu.VMEM((NC * KR, LN), F32),
            pltpu.VMEM((3, NB * KR, LN), F32),
            pltpu.VMEM((NW * KWALL, LN), F32),
            pltpu.VMEM((NC * 32, LN), F32),
            pltpu.VMEM((NW * 16, LN), F32),
            pltpu.VMEM((NC, LN, LN), BF16),
            pltpu.VMEM((NB, LN, 3 * LN), BF16),
            pltpu.VMEM((NW, LN, LN), BF16),
            pltpu.VMEM((NC, 32, 2 * LN), BF16),
            pltpu.VMEM((NW, 16, 2 * LN), BF16),
            pltpu.VMEM((NB, 16, 2 * LN), F32),
            pltpu.VMEM((NB, 8, 2 * LN), F32),
        ],
        **kw,
    )(pairs, wpairs, own, ghosts, walls)


def padded(block, axis, width):
    count = lax.axis_size(axis)
    forward = [(i, i + 1) for i in range(count - 1)]
    backward = [(target, source) for source, target in forward]
    low = lax.ppermute(block[:, block.shape[1] - width :], axis, forward)
    high = lax.ppermute(block[:, :width], axis, backward)
    return jnp.concatenate([low, block, high], axis=1)


def per_device(fluid_state, ghost_list, pair_list, wall_state, wall_count, wall_pairs):
    own_blocks = jnp.transpose(fluid_state.reshape(8, NB, LN), (1, 0, 2))
    outgoing = own_blocks[ghost_list]
    size = lax.axis_size("orb")
    arrived = [
        lax.ppermute(outgoing[q - 1], "orb", [(i, i ^ q) for i in range(size)]) for q in range(1, 8)
    ]
    ghosts = jnp.concatenate(arrived).reshape(-1, LN)
    alive = (jnp.arange(LN, dtype=jnp.int32)[None, :] < wall_count[:, None]).astype(F32).reshape(-1)
    wall_live = jnp.concatenate([wall_state[0:3], wall_state[3:4] * alive[None, :]], axis=0)
    walls = padded(wall_live, "wall", EB * LN)
    rates, acceleration, peak = pair_forces(pair_list, wall_pairs, fluid_state, ghosts, walls)
    peak = lax.pmax(peak[0, 0], ("orb", "wall"))
    time_step = courant * jnp.sqrt(smoothing / (peak + 1e-06))
    return (rates.reshape(-1), acceleration, time_step)


def solution(mesh):
    return jax.shard_map(
        per_device,
        mesh=mesh,
        in_specs=(
            P(None, ("orb", "wall")),
            P(None, ("orb", "wall")),
            P(("orb", "wall"), None),
            P(None, ("orb", "wall")),
            P(("orb", "wall")),
            P(("orb", "wall"), None),
        ),
        out_specs=(P(("orb", "wall")), P(None, ("orb", "wall")), P()),
        check_vma=False,
    )
```

```python
import jax
import jax.numpy as jnp
from jax import lax
from jax.experimental import pallas as pl
from jax.experimental.pallas import tpu as pltpu
from jax.sharding import PartitionSpec as P

NB = 24
K = 14
KW = 4
GH = 6
WB = 6
EB = 1
NC = NB + 7 * GH
NW = WB + 2 * EB
LN = 128

smoothing = 0.1
support = 0.3
kernel_norm = 21.0 / (2.0 * 3.141592653589793 * support**3)
grad_coeff = -20.0 / support**2 * kernel_norm
tait_coeff = 25.0 / 7.0
visc_coeff = 0.05
cohesion = 2000.0
adhesion = 2000.0
gravity = 9.81
courant = 0.25

center = 0.3
inv_support = 1.0 / support
eps_scaled = 0.0001 / support**2
pull_scale = 4.0 * cohesion
wall_pull_scale = 4.0 * adhesion
visc_scaled = visc_coeff * -grad_coeff / support / pull_scale

F32 = jnp.float32
BF16 = jnp.bfloat16


def split(value, terms):
    parts = []
    for _ in range(terms - 1):
        high = value.astype(BF16).astype(F32)
        parts.append(high)
        value = value - high
    parts.append(value.astype(BF16).astype(F32))
    return parts


def pressure_of(density):
    return tait_coeff * (density**7 - 1.0)


def dot3(a, b):
    return a[0] * b[0] + a[1] * b[1] + a[2] * b[2]


CROSS = ((0, 0), (0, 1), (0, 2), (1, 0), (1, 1), (2, 0))


def source_rows(y, v, rho_half):
    ys = [split(c, 3) for c in y]
    norm = split(dot3(y, y), 3)
    one = jnp.ones_like(y[0])
    rows = []
    for c in range(3):
        rows += [ys[c][j] for j, _ in CROSS]
    rows += [one] * 3
    rows += norm
    if v is None:
        return rows
    vs = [split(c, 2) for c in v]
    vt = [c[0] + c[1] for c in vs]
    for c in range(3):
        rows += [vs[c][0], vs[c][0], vs[c][0], vs[c][1], vs[c][1]]
    rows += split(dot3(vt, y), 3)
    rows += [norm[0], norm[0], norm[1]]
    rows += split(rho_half * dot3(y, y), 3)
    hs = split(rho_half, 3)
    rows += [hs[j] for j, _ in CROSS]
    for c in range(3):
        hy = split(rho_half * y[c], 3)
        rows += [hy[j] for j, _ in CROSS]
    return rows


def target_rows(y, v, rho_half):
    ys = [split(c, 3) for c in y]
    vs = [split(c, 2) for c in v]
    vt = [c[0] + c[1] for c in vs]
    sq = dot3(y, y)
    norm = split(sq, 3)
    reach = sq + eps_scaled
    vy = split(dot3(vt, y), 3)
    hs = split(rho_half, 3)
    hn = split(rho_half * reach, 3)
    rs = split(reach, 3)
    one = jnp.ones_like(y[0])
    zero = jnp.zeros_like(y[0])
    rows = []
    for c in range(3):
        hy = split(rho_half * y[c], 3)
        for _, i in CROSS:
            approach = -vs[c][i] if i < 2 else zero
            rows.append((-2.0 * ys[c][i], approach, -2.0 * hy[i]))
    for i in range(3):
        rows.append((norm[i], vy[i], hn[i]))
    for i in range(3):
        rows.append((one, zero, hs[0]))
    for c in range(3):
        for i in (0, 1, 2, 0, 1):
            rows.append((zero, -ys[c][i], zero))
    rows += [(zero, one, zero)] * 3
    rows += [(zero, zero, hs[1]), (zero, zero, hs[2]), (zero, zero, hs[1])]
    rows += [(zero, zero, one)] * 3
    for _, i in CROSS:
        rows.append((zero, zero, rs[i]))
    for c in range(3):
        for _, i in CROSS:
            rows.append((zero, zero, -2.0 * ys[c][i]))
    return rows


KR = 72
KWALL = 24


def column_rows(quantities):
    parts = [split(q, 2) for q in quantities]
    return [p[0] for p in parts], [p[1] for p in parts]


def falloff_of(dist_sq):
    dist_sq = jnp.maximum(dist_sq, 1e-30)
    s = jnp.maximum(1.0 - dist_sq * lax.rsqrt(dist_sq), 0.0)
    return s, s * s * s


def two_terms(value):
    high = value.astype(BF16)
    return high, (value - high.astype(F32)).astype(BF16)


def pair_kernel(
    pair_ref, wpair_ref, own_ref, ghost_ref, wall_ref, rate_ref, accel_ref, peak_ref,
    cand, wcand, jf32, if32, wf32, cl32, wc32, jf, tf, wf, cl, wc, sums, wsums,
    geo0, geo1, wgeo0, wgeo1,
):
    for b in range(NB):
        cand[8 * b : 8 * b + 8, :] = own_ref[:, LN * b : LN * b + LN]
    cand[8 * NB :, :] = ghost_ref[...]
    for b in range(NW):
        wcand[4 * b : 4 * b + 4, :] = wall_ref[:, LN * b : LN * b + LN]

    state = [cand[pl.ds(r, NC, stride=8), :] for r in range(8)]
    y = [(state[c] - center) * inv_support for c in range(3)]
    v = state[3:6]
    rho, mass = state[6], state[7]
    rho_half = (0.5 / visc_scaled) * rho
    push = pressure_of(rho) / (rho * rho)

    rows = source_rows(y, v, rho_half)
    assert len(rows) == KR
    for k, row in enumerate(rows):
        jf32[pl.ds(k, NC, stride=KR), :] = row
    vt = v
    cols = [mass] + [mass * c for c in y] + [mass * c for c in vt]
    cols += [mass * dot3(vt, y), mass * push] + [mass * push * c for c in y]
    high, low = column_rows(cols)
    cl32[...] = jnp.zeros_like(cl32)
    for k in range(12):
        cl32[pl.ds(k, NC, stride=32), :] = high[k]
        cl32[pl.ds(16 + k, NC, stride=32), :] = low[k]

    ty = [c[:NB] for c in y]
    tv = [c[:NB] for c in v]
    weights = target_rows(ty, tv, rho_half[:NB])
    assert len(weights) == KR
    for k, row in enumerate(weights):
        for part in range(3):
            if32[part, pl.ds(k, NB, stride=KR), :] = row[part]

    wstate = [wcand[pl.ds(r, NW, stride=4), :] for r in range(4)]
    wy = [(wstate[c] - center) * inv_support for c in range(3)]
    wrows = source_rows(wy, None, None)
    assert len(wrows) == KWALL
    for k, row in enumerate(wrows):
        wf32[pl.ds(k, NW, stride=KWALL), :] = row
    whigh, wlow = column_rows([wstate[3]] + [wstate[3] * c for c in wy])
    wc32[...] = jnp.zeros_like(wc32)
    for k in range(4):
        wc32[pl.ds(k, NW, stride=16), :] = whigh[k]
        wc32[pl.ds(8 + k, NW, stride=16), :] = wlow[k]

    def build_source(b, carry):
        rows = jf32[pl.ds(b * KR, KR), :]
        rows = jnp.concatenate([rows, jnp.zeros((LN - KR, LN), F32)], axis=0)
        jf[b] = rows.T.astype(BF16)
        c = cl32[pl.ds(b * 32, 32), :].astype(BF16)
        cl[b] = jnp.concatenate([c, c], axis=1)
        return carry

    lax.fori_loop(0, NC, build_source, 0, unroll=6)

    def build_target(b, carry):
        for part in range(3):
            rows = if32[part, pl.ds(b * KR, KR), :]
            rows = jnp.concatenate([rows, jnp.zeros((LN - KR, LN), F32)], axis=0)
            tf[b, :, LN * part : LN * part + LN] = rows.astype(BF16)
        return carry

    lax.fori_loop(0, NB, build_target, 0)

    def build_wall(b, carry):
        rows = wf32[pl.ds(b * KWALL, KWALL), :]
        rows = jnp.concatenate([rows, jnp.zeros((LN - KWALL, LN), F32)], axis=0)
        wf[b] = rows.T.astype(BF16)
        c = wc32[pl.ds(b * 16, 16), :].astype(BF16)
        wc[b] = jnp.concatenate([c, c], axis=1)
        return carry

    lax.fori_loop(0, NW, build_wall, 0)

    def geometry(b, geo, wgeo):
        weights = tf[b]
        lhs = jnp.concatenate([jf[pair_ref[k, b]] for k in range(K)], axis=0)
        geo[...] = jnp.dot(lhs, weights, preferred_element_type=F32)
        lhs = jnp.concatenate([wf[wpair_ref[k, b]] for k in range(KW)], axis=0)
        wgeo[...] = jnp.dot(lhs, weights[:, :LN], preferred_element_type=F32)

    def summed(columns, cubed, pull):
        sh, sl = two_terms(cubed)
        uh, ul = two_terms(pull)
        mat = jnp.concatenate(
            [jnp.concatenate([sh, uh], axis=1), jnp.concatenate([sl, ul], axis=1)], axis=0
        )
        return jnp.dot(columns, mat, preferred_element_type=F32)

    def forces(b, geo, wgeo):
        total = jnp.zeros((32, 2 * LN), F32)
        for k in range(K):
            tile = pl.ds(k * LN, LN)
            s, cubed = falloff_of(geo[tile, :LN])
            root = lax.rsqrt(geo[tile, 2 * LN :])
            drag = jnp.minimum(geo[tile, LN : 2 * LN], 0.0) * (root * root)
            total += summed(cl[pair_ref[k, b]], cubed, cubed * (drag - s))
        sums[b] = total[:16] + total[16:]
        total = jnp.zeros((16, 2 * LN), F32)
        for k in range(KW):
            s, cubed = falloff_of(wgeo[pl.ds(k * LN, LN), :])
            total += summed(wc[wpair_ref[k, b]], cubed, cubed * s)
        wsums[b] = total[:8] + total[8:]

    geometry(0, geo0, wgeo0)

    def two_blocks(t, carry):
        b = 2 * t
        geometry(b + 1, geo1, wgeo1)
        forces(b, geo0, wgeo0)
        geometry(jnp.minimum(b + 2, NB - 1), geo0, wgeo0)
        forces(b + 1, geo1, wgeo1)
        return carry

    lax.fori_loop(0, NB // 2, two_blocks, 0)

    def take(ref, row, lane):
        return ref[:, row, lane : lane + LN]

    spart = [take(sums, r, 0) for r in range(12)]
    upart = [take(sums, r, LN) for r in range(4)]
    wspart = [take(wsums, r, 0) for r in range(4)]
    wupart = [take(wsums, r, LN) for r in range(4)]
    own_push = push[:NB]
    rate = (
        dot3(tv, ty) * (spart[0] + wspart[0])
        - dot3(tv, [spart[1 + c] + wspart[1 + c] for c in range(3)])
        - dot3(spart[4:7], ty)
        + spart[7]
    )
    rate_ref[...] = (grad_coeff * support) * rate
    square = jnp.zeros((NB, LN), F32)
    for c in range(3):
        pressed = own_push * (
            ty[c] * (spart[0] + 2.0 * wspart[0]) - (spart[1 + c] + 2.0 * wspart[1 + c])
        )
        pressed += ty[c] * spart[8] - spart[9 + c]
        near = ty[c] * spart[0] - spart[1 + c]
        wnear = ty[c] * wspart[0] - wspart[1 + c]
        pulled = 3.0 * cohesion * near + pull_scale * (ty[c] * upart[0] - upart[1 + c])
        pulled += 3.0 * adhesion * wnear - wall_pull_scale * (ty[c] * wupart[0] - wupart[1 + c])
        force = (-grad_coeff * support) * pressed - support * pulled
        if c == 2:
            force = force - gravity
        square += force * force
        for b in range(NB):
            accel_ref[c : c + 1, LN * b : LN * b + LN] = force[b : b + 1]
    peak = jnp.max(jnp.sqrt(square), axis=0, keepdims=True)
    peak_ref[...] = jnp.broadcast_to(jnp.max(peak, axis=1, keepdims=True), (8, LN))


def pair_forces(pairs, wpairs, own, ghosts, walls, **kw):
    vmem = pl.BlockSpec(memory_space=pltpu.VMEM)
    smem = pl.BlockSpec(memory_space=pltpu.SMEM)
    return pl.pallas_call(
        pair_kernel,
        name="pair_forces",
        out_shape=(
            jax.ShapeDtypeStruct((NB, LN), F32),
            jax.ShapeDtypeStruct((3, NB * LN), F32),
            jax.ShapeDtypeStruct((8, LN), F32),
        ),
        in_specs=[smem, smem, vmem, vmem, vmem],
        out_specs=(vmem, vmem, vmem),
        scratch_shapes=[
            pltpu.VMEM((NC * 8, LN), F32),
            pltpu.VMEM((NW * 4, LN), F32),
            pltpu.VMEM((NC * KR, LN), F32),
            pltpu.VMEM((3, NB * KR, LN), F32),
            pltpu.VMEM((NW * KWALL, LN), F32),
            pltpu.VMEM((NC * 32, LN), F32),
            pltpu.VMEM((NW * 16, LN), F32),
            pltpu.VMEM((NC, LN, LN), BF16),
            pltpu.VMEM((NB, LN, 3 * LN), BF16),
            pltpu.VMEM((NW, LN, LN), BF16),
            pltpu.VMEM((NC, 32, 2 * LN), BF16),
            pltpu.VMEM((NW, 16, 2 * LN), BF16),
            pltpu.VMEM((NB, 16, 2 * LN), F32),
            pltpu.VMEM((NB, 8, 2 * LN), F32),
            pltpu.VMEM((K * LN, 3 * LN), F32),
            pltpu.VMEM((K * LN, 3 * LN), F32),
            pltpu.VMEM((KW * LN, LN), F32),
            pltpu.VMEM((KW * LN, LN), F32),
        ],
        **kw,
    )(pairs, wpairs, own, ghosts, walls)


MESH = pl.DeviceIdType.MESH


def flipped(place, pattern):
    partner = place
    for bit in (1, 2, 4):
        if pattern & bit:
            partner = partner + bit - 2 * bit * lax.rem(lax.div(place, bit), 2)
    return partner


def exchange_kernel(
    ghost_ref, count_ref, own_ref, wall_ref, ghosts_ref, walls_ref,
    blocks, outgoing, edges, edges_in, send_sems, recv_sems,
):
    orb = lax.axis_index("orb")
    place = lax.axis_index("wall")
    places = lax.axis_size("wall")
    partners = [flipped(orb, q) for q in range(1, 8)]
    above, below = lax.rem(place + 1, places), lax.rem(place + places - 1, places)

    barrier = pltpu.get_barrier_semaphore()
    for partner in partners:
        pl.semaphore_signal(barrier, inc=1, device_id={"orb": partner}, device_id_type=MESH)
    for partner in (above, below):
        pl.semaphore_signal(barrier, inc=1, device_id={"wall": partner}, device_id_type=MESH)

    lane = lax.broadcasted_iota(jnp.int32, (1, LN), 1)
    for b in range(WB):
        block = wall_ref[:, LN * b : LN * b + LN]
        live = jnp.where(lane < count_ref[b], block[3:4], 0.0)
        block = jnp.concatenate([block[:3], live], axis=0)
        walls_ref[:, LN * (b + 1) : LN * (b + 2)] = block
        if b == 0:
            edges[0] = block
        if b == WB - 1:
            edges[1] = block
    for b in range(NB):
        blocks[b] = own_ref[:, LN * b : LN * b + LN]
    for q in range(7):
        for g in range(GH):
            outgoing[q, 8 * g : 8 * g + 8, :] = blocks[ghost_ref[q, g]]

    pl.semaphore_wait(barrier, 9)
    copies = []
    for slot, partner in enumerate((below, above)):
        copies.append(
            pltpu.make_async_remote_copy(
                src_ref=edges.at[slot],
                dst_ref=edges_in.at[slot],
                send_sem=send_sems.at[7 + slot],
                recv_sem=recv_sems.at[7 + slot],
                device_id={"wall": partner},
                device_id_type=MESH,
            )
        )
    rows = 8 * GH
    for q in (6, 5, 3, 4, 2, 1, 0):
        copies.append(
            pltpu.make_async_remote_copy(
                src_ref=outgoing.at[q],
                dst_ref=ghosts_ref.at[pl.ds(q * rows, rows)],
                send_sem=send_sems.at[q],
                recv_sem=recv_sems.at[q],
                device_id={"orb": partners[q]},
                device_id_type=MESH,
            )
        )
    for copy in copies:
        copy.start()
    for copy in copies[:2]:
        copy.wait()
    walls_ref[:, :LN] = jnp.where(place > 0, edges_in[1], 0.0)
    walls_ref[:, LN * (NW - 1) :] = jnp.where(place < places - 1, edges_in[0], 0.0)
    for copy in copies[2:]:
        copy.wait()


def exchange(ghost_list, wall_count, own, walls):
    vmem = pl.BlockSpec(memory_space=pltpu.VMEM)
    smem = pl.BlockSpec(memory_space=pltpu.SMEM)
    return pl.pallas_call(
        exchange_kernel,
        name="exchange",
        out_shape=(
            jax.ShapeDtypeStruct((7 * GH * 8, LN), F32),
            jax.ShapeDtypeStruct((4, NW * LN), F32),
        ),
        in_specs=[smem, smem, vmem, vmem],
        out_specs=(vmem, vmem),
        scratch_shapes=[
            pltpu.VMEM((NB, 8, LN), F32),
            pltpu.VMEM((7, GH * 8, LN), F32),
            pltpu.VMEM((2, 4, LN), F32),
            pltpu.VMEM((2, 4, LN), F32),
            pltpu.SemaphoreType.DMA((9,)),
            pltpu.SemaphoreType.DMA((9,)),
        ],
        compiler_params=pltpu.CompilerParams(collective_id=0, has_side_effects=True),
    )(ghost_list, wall_count, own, walls)


def rounds():
    orb = lax.axis_index("orb")
    place = lax.axis_index("wall")
    x, rest = lax.div(orb, 16), lax.rem(orb, 16)
    mine = x * 4 + place
    first = []
    for t in range(1, 16):
        other = lax.rem(mine + t, 16)
        first.append({"orb": lax.div(other, 4) * 16 + rest, "wall": lax.rem(other, 4)})
    second = [{"orb": x * 16 + lax.rem(rest + t, 16), "wall": place} for t in range(1, 16)]
    return first, second


def peak_kernel(peak_ref, step_ref, held, slots, send_sems, recv_sems):
    phases = rounds()
    barrier = pltpu.get_barrier_semaphore()
    for phase in phases:
        for partner in phase:
            pl.semaphore_signal(barrier, inc=1, device_id=partner, device_id_type=MESH)
    held[0] = peak_ref[0:1, :]
    pl.semaphore_wait(barrier, 30)
    for n, phase in enumerate(phases):
        copies = [
            pltpu.make_async_remote_copy(
                src_ref=held.at[n],
                dst_ref=slots.at[n, t],
                send_sem=send_sems.at[n, t],
                recv_sem=recv_sems.at[n, t],
                device_id=partner,
                device_id_type=MESH,
            )
            for t, partner in enumerate(phase)
        ]
        for copy in copies:
            copy.start()
        best = held[n]
        for t, copy in enumerate(copies):
            copy.wait()
            best = jnp.maximum(best, slots[n, t])
        held[n + 1] = best
    step = courant * jnp.sqrt(smoothing / (best + 1e-06))
    step_ref[0, 0] = jnp.max(step)


def global_step(peak):
    return pl.pallas_call(
        peak_kernel,
        name="global_step",
        out_shape=jax.ShapeDtypeStruct((1, 1), F32),
        in_specs=[pl.BlockSpec(memory_space=pltpu.VMEM)],
        out_specs=pl.BlockSpec(memory_space=pltpu.SMEM),
        scratch_shapes=[
            pltpu.VMEM((3, 1, LN), F32),
            pltpu.VMEM((2, 15, 1, LN), F32),
            pltpu.SemaphoreType.DMA((2, 15)),
            pltpu.SemaphoreType.DMA((2, 15)),
        ],
        compiler_params=pltpu.CompilerParams(collective_id=1, has_side_effects=True),
    )(peak)


def per_device(fluid_state, ghost_list, pair_list, wall_state, wall_count, wall_pairs):
    ghosts, walls = exchange(ghost_list, wall_count, fluid_state, wall_state)
    rates, acceleration, peak = pair_forces(pair_list.T, wall_pairs.T, fluid_state, ghosts, walls)
    step = global_step(peak)
    return (rates.reshape(-1), acceleration, step.reshape(()))


def solution(mesh):
    return jax.shard_map(
        per_device,
        mesh=mesh,
        in_specs=(
            P(None, ("orb", "wall")),
            P(None, ("orb", "wall")),
            P(("orb", "wall"), None),
            P(None, ("orb", "wall")),
            P(("orb", "wall")),
            P(("orb", "wall"), None),
        ),
        out_specs=(P(("orb", "wall")), P(None, ("orb", "wall")), P()),
        check_vma=False,
    )
```

```python
import jax
import jax.numpy as jnp
from jax import lax
from jax.experimental import pallas as pl
from jax.experimental.pallas import tpu as pltpu
from jax.sharding import PartitionSpec as P

NB = 24
K = 14
KW = 4
GH = 6
WB = 6
EB = 1
NC = NB + 7 * GH
NW = WB + 2 * EB
LN = 128

smoothing = 0.1
support = 0.3
kernel_norm = 21.0 / (2.0 * 3.141592653589793 * support**3)
grad_coeff = -20.0 / support**2 * kernel_norm
tait_coeff = 25.0 / 7.0
visc_coeff = 0.05
cohesion = 2000.0
adhesion = 2000.0
gravity = 9.81
courant = 0.25

center = 0.3
inv_support = 1.0 / support
eps_scaled = 0.0001 / support**2
pull_scale = 4.0 * cohesion
wall_pull_scale = 4.0 * adhesion
visc_scaled = visc_coeff * -grad_coeff / support / pull_scale
half_scale = 0.5 / visc_scaled

F32 = jnp.float32
BF16 = jnp.bfloat16


def split(value):
    parts = []
    for _ in range(2):
        high = value.astype(BF16).astype(F32)
        parts.append(high)
        value = value - high
    parts.append(value.astype(BF16).astype(F32))
    return parts


def two_terms(value):
    high = value.astype(BF16)
    return high, (value - high.astype(F32)).astype(BF16)


def pressure_of(density):
    return tait_coeff * (density**7 - 1.0)


def dot3(a, b):
    return a[0] * b[0] + a[1] * b[1] + a[2] * b[2]


def rows_of(block):
    return [block[c : c + 1] for c in range(block.shape[0])]


def stack(rows):
    return jnp.concatenate(rows, axis=0)


CROSS = ((0, 0), (0, 1), (0, 2), (1, 0), (1, 1), (2, 0))


def scaled_rows(block):
    rows = rows_of(block)
    y = [(row - center) * inv_support for row in rows[:3]]
    return y, rows[3:6], rows[6], rows[7]


def wide(groups):
    rows = stack(groups)
    spare = LN - rows.shape[0]
    return stack([rows, jnp.zeros((spare, LN), F32)]) if spare else rows


def source_tiles(block):
    y, v, rho, mass = scaled_rows(block)
    half = half_scale * rho
    one, zero = jnp.ones_like(mass), jnp.zeros_like(mass)
    norm, flow = dot3(y, y), dot3(v, y)
    terms = split(stack(y + v + [half, zero]))
    sums = split(stack([norm, flow, one, one, one, zero, zero, zero]))
    mixed = split(stack([half * c for c in y] + [half * norm, norm, one, one, one]))
    base = [terms[j] for j, _ in CROSS]
    push = pressure_of(rho) / (rho * rho)
    heavy = stack(y + v + [flow, one]) * mass
    pushed = heavy * push
    hh, hl = two_terms(heavy)
    ph, pl_ = two_terms(pushed)
    return wide(base + sums), wide(base + [mixed[j] for j, _ in CROSS]), stack([hh, ph, hl, pl_])


def wall_tiles(block):
    rows = rows_of(block)
    y = [(row - center) * inv_support for row in rows[:3]]
    mass = rows[3]
    one, zero = jnp.ones_like(mass), jnp.zeros_like(mass)
    terms = split(stack(y + [zero] * 5))
    sums = split(stack([dot3(y, y), zero, one, one, one, zero, zero, zero]))
    heavy = stack(y + [one, zero, zero, zero, zero]) * mass
    hh, hl = two_terms(heavy)
    return wide([terms[j] for j, _ in CROSS] + sums), stack([hh, hl])


def target_tiles(block):
    y, v, rho, mass = scaled_rows(block)
    half = half_scale * rho
    one, zero = jnp.ones_like(mass), jnp.zeros_like(mass)
    norm, flow = dot3(y, y), dot3(v, y)
    reach = norm + eps_scaled
    twice = [-2.0 * c for c in y]
    far = split(stack(twice + [zero] * 5))
    near = split(stack([-c for c in v] + [-c for c in y] + [zero] * 2))
    damp = split(stack([half * c for c in twice] + [zero] * 3 + [reach, zero]))
    mixed = split(stack(twice + [zero, half] + [zero] * 3))
    norms, flows, grounds = split(norm), split(flow), split(half * reach)
    mixed[0] = mixed[0] + stack([zero] * 3 + [one, zero] + grounds)
    far_sum = stack([one, zero] + norms + [zero] * 3)
    near_sum = stack([zero, one] + flows + [zero] * 3)
    return (
        wide([far[i] for _, i in CROSS] + [far_sum] * 3),
        wide([near[i] for _, i in CROSS] + [near_sum] * 3),
        wide([damp[i] for _, i in CROSS] + [mixed[i] for _, i in CROSS]),
    )


def falloff_of(dist_sq):
    dist_sq = jnp.maximum(dist_sq, 1e-30)
    s = jnp.maximum(1.0 - dist_sq * lax.rsqrt(dist_sq), 0.0)
    return s, s * s * s


def product(left, right):
    return jnp.dot(left, right, preferred_element_type=F32)


MESH = pl.DeviceIdType.MESH


def flipped(place, pattern):
    partner = place
    for bit in (1, 2, 4):
        if pattern & bit:
            partner = partner + bit - 2 * bit * lax.rem(lax.div(place, bit), 2)
    return partner


def rounds():
    orb = lax.axis_index("orb")
    place = lax.axis_index("wall")
    x, rest = lax.div(orb, 16), lax.rem(orb, 16)
    mine = x * 4 + place
    first = []
    for t in range(1, 16):
        other = lax.rem(mine + t, 16)
        first.append({"orb": lax.div(other, 4) * 16 + rest, "wall": lax.rem(other, 4)})
    second = [{"orb": x * 16 + lax.rem(rest + t, 16), "wall": place} for t in range(1, 16)]
    return first, second


def send(source, target, send_sem, recv_sem, device):
    return pltpu.make_async_remote_copy(
        src_ref=source,
        dst_ref=target,
        send_sem=send_sem,
        recv_sem=recv_sem,
        device_id=device,
        device_id_type=MESH,
    )


def step_kernel(
    pair_ref, wpair_ref, ghost_ref, count_ref, own_ref, wall_ref, rate_ref, accel_ref, step_ref,
    blocks, outgoing, arrived, edges, edges_in, held, slots,
    sf, se, sc, wf, wc, tf, te, tw, sums, wsums,
    near0, near1, damp0, damp1, wall0, wall1, own_rows,
    send_sems, recv_sems, peak_send, peak_recv,
):
    orb = lax.axis_index("orb")
    place = lax.axis_index("wall")
    places = lax.axis_size("wall")
    partners = [{"orb": flipped(orb, q)} for q in range(1, 8)]
    above = {"wall": lax.rem(place + 1, places)}
    below = {"wall": lax.rem(place + places - 1, places)}
    phases = rounds()

    barrier = pltpu.get_barrier_semaphore()
    greeted = [*partners, above, below, *phases[0], *phases[1]]
    for device in greeted:
        pl.semaphore_signal(barrier, inc=1, device_id=device, device_id_type=MESH)

    for b in range(NB):
        blocks[b] = own_ref[:, LN * b : LN * b + LN]
    for q in range(7):
        for g in range(GH):
            outgoing[q, 8 * g : 8 * g + 8, :] = blocks[ghost_ref[q, g]]
    lane_row = lax.broadcasted_iota(jnp.int32, (1, LN), 1)

    def live_block(b):
        block = wall_ref[:, LN * b : LN * b + LN]
        return stack([block[:3], jnp.where(lane_row < count_ref[b], block[3:4], 0.0)])

    edges[0] = live_block(0)
    edges[1] = live_block(WB - 1)

    row = lax.broadcasted_iota(jnp.int32, (LN, 2 * LN), 0)
    lane = lax.broadcasted_iota(jnp.int32, (LN, 2 * LN), 1)
    doubled = jnp.where(row == lane // 32 * 16 + lane % 16, 1.0, 0.0).astype(BF16)

    def keep_source(j, block):
        geometry, damping, columns = source_tiles(block)
        sf[j] = geometry.astype(BF16).T
        se[j] = damping.astype(BF16).T
        sc[j] = product(columns, doubled).astype(BF16)

    def build_own(b, carry):
        keep_source(b, blocks[b])
        return carry

    def keep_wall(b, block):
        geometry, columns = wall_tiles(block)
        wf[b] = geometry.astype(BF16).T
        wc[b] = product(columns, doubled).astype(BF16)

    def build_target(b, carry):
        distance, approach, damping = [t.astype(BF16) for t in target_tiles(blocks[b])]
        zero = jnp.zeros((LN, LN), BF16)
        tf[b] = jnp.concatenate([distance, approach], axis=1)
        for ref, tile in ((te, damping), (tw, distance)):
            ref[b, :LN, :LN] = tile
            ref[b, :LN, LN:] = zero
            ref[b, LN:, :LN] = zero
            ref[b, LN:, LN:] = tile
        return carry

    lax.fori_loop(0, NB, build_target, 0, unroll=2)
    for b in range(WB):
        keep_wall(b + 1, live_block(b))

    pl.semaphore_wait(barrier, len(greeted))
    edge_copies = [
        send(edges.at[n], edges_in.at[n], send_sems.at[7 + n], recv_sems.at[7 + n], device)
        for n, device in enumerate((below, above))
    ]
    ghost_copies = [
        send(outgoing.at[q], arrived.at[q], send_sems.at[q], recv_sems.at[q], partners[q])
        for q in range(7)
    ]
    for copy in edge_copies:
        copy.start()
    for q in (6, 5, 3, 4, 2, 1, 0):
        ghost_copies[q].start()

    lax.fori_loop(0, NB, build_own, 0, unroll=3)
    for copy in edge_copies:
        copy.wait()
    keep_wall(0, jnp.where(place > 0, edges_in[1], 0.0))
    keep_wall(NW - 1, jnp.where(place < places - 1, edges_in[0], 0.0))

    def gathered(ref, indices):
        return stack([ref[j] for j in indices])

    def paired(ref, indices):
        return jnp.concatenate([gathered(ref, indices[0::2]), gathered(ref, indices[1::2])], axis=1)

    def matrix(cubed, pull):
        terms = two_terms(cubed), two_terms(pull)
        rows = []
        for top in range(0, LN, 16):
            for part in range(2):
                rows.append(jnp.concatenate([t[part][top : top + 16] for t in terms], axis=1))
        return stack(rows)

    group = 4
    tall = KW // 2 * LN

    def wall_geometry(t, wall):
        for n in range(group):
            b = t * group + n
            tiles = paired(wf, [wpair_ref[k, b] for k in range(KW)])
            wall[n * tall : (n + 1) * tall] = product(tiles, tw[b])

    def wall_forces(t, wall):
        for n in range(group):
            b = t * group + n
            total = jnp.zeros((16, 2 * LN), F32)
            for k in range(KW):
                half, side = pl.ds(n * tall + k // 2 * LN, LN), k % 2 * LN
                s, cubed = falloff_of(wall[half, side : side + LN])
                total += product(wc[wpair_ref[k, b]], matrix(cubed, cubed * s))
            wsums[b] = total[:8] + total[8:]

    wall_geometry(0, wall0)

    def two_walls(t, carry):
        wall_geometry(2 * t + 1, wall1)
        wall_forces(2 * t, wall0)
        wall_geometry(jnp.minimum(2 * t + 2, NB // group - 1), wall0)
        wall_forces(2 * t + 1, wall1)
        return carry

    lax.fori_loop(0, NB // group // 2, two_walls, 0)

    for q in (0, 1, 2, 4, 3, 5, 6):
        ghost_copies[q].wait()

        def build_ghost(g, carry, q=q):
            keep_source(NB + q * GH + g, arrived[q, pl.ds(pl.multiple_of(g * 8, 8), 8), :])
            return carry

        lax.fori_loop(0, GH, build_ghost, 0, unroll=3)

    def geometry(b, near, damp):
        indices = [pair_ref[k, b] for k in range(K)]
        near[...] = product(gathered(sf, indices), tf[b])
        damp[...] = product(paired(se, indices), te[b])

    def forces(b, near, damp):
        total = jnp.zeros((32, 2 * LN), F32)
        for k in range(K):
            tile, half, side = pl.ds(k * LN, LN), pl.ds(k // 2 * LN, LN), k % 2 * LN
            s, cubed = falloff_of(near[tile, :LN])
            root = lax.rsqrt(damp[half, side : side + LN])
            drag = jnp.minimum(near[tile, LN:], 0.0) * (root * root)
            total += product(sc[pair_ref[k, b]], matrix(cubed, cubed * (drag - s)))
        sums[b] = total[:16] + total[16:]

    geometry(0, near0, damp0)

    def two_blocks(t, carry):
        b = 2 * t
        geometry(b + 1, near1, damp1)
        forces(b, near0, damp0)
        geometry(jnp.minimum(b + 2, NB - 1), near0, damp0)
        forces(b + 1, near1, damp1)
        return carry

    lax.fori_loop(0, NB // 2, two_blocks, 0)

    for b in range(NB):
        own_rows[8 * b : 8 * b + 8, :] = blocks[b]
    state = [own_rows[pl.ds(r, NB, stride=8), :] for r in range(8)]
    y = [(r - center) * inv_support for r in state[:3]]
    v, rho = state[3:6], state[6]
    push = pressure_of(rho) / (rho * rho)
    weigh = [sums[:, r, :LN] for r in range(16)]
    pull = [sums[:, r, LN:] for r in range(16)]
    wweigh = [wsums[:, r, :LN] for r in range(4)]
    wpull = [wsums[:, r, LN:] for r in range(4)]
    square = jnp.zeros((NB, LN), F32)
    forces_out = []
    for c in range(3):
        near = y[c] * weigh[7] - weigh[c]
        wnear = y[c] * wweigh[3] - wweigh[c]
        pressed = push * (near + 2.0 * wnear) + y[c] * weigh[15] - weigh[8 + c]
        pulled = 3.0 * cohesion * near + pull_scale * (y[c] * pull[7] - pull[c])
        pulled += 3.0 * adhesion * wnear - wall_pull_scale * (y[c] * wpull[3] - wpull[c])
        force = (-grad_coeff * support) * pressed - support * pulled
        if c == 2:
            force = force - gravity
        square += force * force
        forces_out.append(force)
    best = jnp.max(jnp.max(square, axis=0, keepdims=True), axis=1, keepdims=True)
    held[0] = jnp.broadcast_to(jnp.sqrt(best), (1, LN))

    def phase_copies(n):
        return [
            send(held.at[n], slots.at[n, t], peak_send.at[n, t], peak_recv.at[n, t], device)
            for t, device in enumerate(phases[n])
        ]

    copies = phase_copies(0)
    for copy in copies:
        copy.start()
    rate = (
        dot3(v, y) * (weigh[7] + wweigh[3])
        - dot3(v, [weigh[c] + wweigh[c] for c in range(3)])
        - dot3(weigh[3:6], y)
        + weigh[6]
    )
    rate_ref[...] = (grad_coeff * support) * rate
    for c in range(3):
        for b in range(NB):
            accel_ref[c : c + 1, LN * b : LN * b + LN] = forces_out[c][b : b + 1]
    for n in range(2):
        best = held[n]
        for t, copy in enumerate(copies):
            copy.wait()
            best = jnp.maximum(best, slots[n, t])
        held[n + 1] = best
        if n == 0:
            copies = phase_copies(1)
            for copy in copies:
                copy.start()
    step_ref[0, 0] = jnp.max(courant * jnp.sqrt(smoothing / (best + 1e-06)))


def per_device(fluid_state, ghost_list, pair_list, wall_state, wall_count, wall_pairs):
    vmem = pl.BlockSpec(memory_space=pltpu.VMEM)
    smem = pl.BlockSpec(memory_space=pltpu.SMEM)
    rates, acceleration, step = pl.pallas_call(
        step_kernel,
        name="step",
        out_shape=(
            jax.ShapeDtypeStruct((NB, LN), F32),
            jax.ShapeDtypeStruct((3, NB * LN), F32),
            jax.ShapeDtypeStruct((1, 1), F32),
        ),
        in_specs=[smem, smem, smem, smem, vmem, vmem],
        out_specs=(vmem, vmem, smem),
        scratch_shapes=[
            pltpu.VMEM((NB, 8, LN), F32),
            pltpu.VMEM((7, GH * 8, LN), F32),
            pltpu.VMEM((7, GH * 8, LN), F32),
            pltpu.VMEM((2, 4, LN), F32),
            pltpu.VMEM((2, 4, LN), F32),
            pltpu.VMEM((3, 1, LN), F32),
            pltpu.VMEM((2, 15, 1, LN), F32),
            pltpu.VMEM((NC, LN, LN), BF16),
            pltpu.VMEM((NC, LN, LN), BF16),
            pltpu.VMEM((NC, 32, 2 * LN), BF16),
            pltpu.VMEM((NW, LN, LN), BF16),
            pltpu.VMEM((NW, 16, 2 * LN), BF16),
            pltpu.VMEM((NB, LN, 2 * LN), BF16),
            pltpu.VMEM((NB, 2 * LN, 2 * LN), BF16),
            pltpu.VMEM((NB, 2 * LN, 2 * LN), BF16),
            pltpu.VMEM((NB, 16, 2 * LN), F32),
            pltpu.VMEM((NB, 8, 2 * LN), F32),
        ]
        + [pltpu.VMEM((K * LN, 2 * LN), F32)] * 2
        + [pltpu.VMEM((K // 2 * LN, 2 * LN), F32)] * 2
        + [pltpu.VMEM((4 * KW // 2 * LN, 2 * LN), F32)] * 2
        + [
            pltpu.VMEM((NB * 8, LN), F32),
            pltpu.SemaphoreType.DMA((9,)),
            pltpu.SemaphoreType.DMA((9,)),
            pltpu.SemaphoreType.DMA((2, 15)),
            pltpu.SemaphoreType.DMA((2, 15)),
        ],
        compiler_params=pltpu.CompilerParams(collective_id=0, has_side_effects=True),
    )(pair_list.T, wall_pairs.T, ghost_list, wall_count, fluid_state, wall_state)
    return (rates.reshape(-1), acceleration, step.reshape(()))


def solution(mesh):
    return jax.shard_map(
        per_device,
        mesh=mesh,
        in_specs=(
            P(None, ("orb", "wall")),
            P(None, ("orb", "wall")),
            P(("orb", "wall"), None),
            P(None, ("orb", "wall")),
            P(("orb", "wall")),
            P(("orb", "wall"), None),
        ),
        out_specs=(P(("orb", "wall")), P(None, ("orb", "wall")), P()),
        check_vma=False,
    )
```

```python
import jax
import jax.numpy as jnp
from jax import lax
from jax.experimental import pallas as pl
from jax.experimental.pallas import tpu as pltpu
from jax.sharding import PartitionSpec as P

NB = 24
K = 14
KW = 4
GH = 6
WB = 6
EB = 1
NC = NB + 7 * GH
NW = WB + 2 * EB
LN = 128
UNROLL = 4
GROUP = 2

smoothing = 0.1
support = 0.3
kernel_norm = 21.0 / (2.0 * 3.141592653589793 * support**3)
grad_coeff = -20.0 / support**2 * kernel_norm
tait_coeff = 25.0 / 7.0
visc_coeff = 0.05
cohesion = 2000.0
adhesion = 2000.0
gravity = 9.81
courant = 0.25

center = 0.3
inv_support = 1.0 / support
eps_scaled = 0.0001 / support**2
pull_scale = 4.0 * cohesion
wall_pull_scale = 4.0 * adhesion
visc_scaled = visc_coeff * -grad_coeff / support / pull_scale
half_scale = 0.5 / visc_scaled

F32 = jnp.float32
BF16 = jnp.bfloat16


def split(value):
    parts = []
    for _ in range(2):
        high = value.astype(BF16).astype(F32)
        parts.append(high)
        value = value - high
    parts.append(value.astype(BF16).astype(F32))
    return parts


def two_terms(value):
    high = value.astype(BF16)
    return high, (value - high.astype(F32)).astype(BF16)


def pressure_of(density):
    return tait_coeff * (density**7 - 1.0)


def dot3(a, b):
    return a[0] * b[0] + a[1] * b[1] + a[2] * b[2]


def rows_of(block):
    return [block[c : c + 1] for c in range(block.shape[0])]


def stack(rows):
    return jnp.concatenate(rows, axis=0)


CROSS = ((0, 0), (0, 1), (0, 2), (1, 0), (1, 1), (2, 0))


def scaled_rows(block):
    rows = rows_of(block)
    y = [(row - center) * inv_support for row in rows[:3]]
    return y, rows[3:6], rows[6], rows[7]


def wide(groups):
    rows = stack(groups)
    spare = LN - rows.shape[0]
    return stack([rows, jnp.zeros((spare, LN), F32)]) if spare else rows


def source_tiles(block):
    y, v, rho, mass = scaled_rows(block)
    half = half_scale * rho
    one, zero = jnp.ones_like(mass), jnp.zeros_like(mass)
    norm, flow = dot3(y, y), dot3(v, y)
    terms = split(stack(y + v + [half, zero]))
    sums = split(stack([norm, flow, one, one, one, zero, zero, zero]))
    push = pressure_of(rho) / (rho * rho)
    heavy = stack(y + v + [flow, one]) * mass
    pushed = heavy * push
    hh, hl = two_terms(heavy)
    ph, pl_ = two_terms(pushed)
    return wide([terms[j] for j, _ in CROSS] + sums), stack([hh, ph, hl, pl_])


def wall_tiles(block):
    rows = rows_of(block)
    y = [(row - center) * inv_support for row in rows[:3]]
    mass = rows[3]
    one, zero = jnp.ones_like(mass), jnp.zeros_like(mass)
    terms = split(stack(y + [zero] * 5))
    sums = split(stack([dot3(y, y), zero, one, one, one, zero, zero, zero]))
    heavy = stack(y + [one, zero, zero, zero, zero]) * mass
    hh, hl = two_terms(heavy)
    return wide([terms[j] for j, _ in CROSS] + sums), stack([hh, hl])


def target_tiles(block):
    y, v, _, mass = scaled_rows(block)
    one, zero = jnp.ones_like(mass), jnp.zeros_like(mass)
    norm, flow = dot3(y, y), dot3(v, y)
    far = split(stack([-2.0 * c for c in y] + [zero] * 5))
    near = split(stack([-c for c in v] + [-c for c in y] + [zero] * 2))
    far_sum = stack([one, zero] + split(norm) + [zero] * 3)
    near_sum = stack([zero, one] + split(flow) + [zero] * 3)
    return (
        wide([far[i] for _, i in CROSS] + [far_sum] * 3),
        wide([near[i] for _, i in CROSS] + [near_sum] * 3),
    )


def falloff_of(dist_sq):
    s = jnp.maximum(1.0 - dist_sq * lax.rsqrt(dist_sq), 0.0)
    return s, s * s * s


def product(left, right):
    return jnp.dot(left, right, preferred_element_type=F32)


MESH = pl.DeviceIdType.MESH


def flipped(place, pattern):
    partner = place
    for bit in (1, 2, 4):
        if pattern & bit:
            partner = partner + bit - 2 * bit * lax.rem(lax.div(place, bit), 2)
    return partner


def rounds():
    orb = lax.axis_index("orb")
    place = lax.axis_index("wall")
    x, rest = lax.div(orb, 16), lax.rem(orb, 16)
    mine = x * 4 + place
    first = []
    for t in range(1, 16):
        other = lax.rem(mine + t, 16)
        first.append({"orb": lax.div(other, 4) * 16 + rest, "wall": lax.rem(other, 4)})
    second = [{"orb": x * 16 + lax.rem(rest + t, 16), "wall": place} for t in range(1, 16)]
    return first, second


def send(source, target, send_sem, recv_sem, device):
    return pltpu.make_async_remote_copy(
        src_ref=source,
        dst_ref=target,
        send_sem=send_sem,
        recv_sem=recv_sem,
        device_id=device,
        device_id_type=MESH,
    )


def step_kernel(
    pair_ref, wpair_ref, ghost_ref, count_ref, own_ref, wall_ref, rate_ref, accel_ref, step_ref,
    blocks, outgoing, arrived, edges, edges_in, held, slots,
    sf, sh, sc, wf, wc, tf, sums, wsums,
    near0, near1, wall0, wall1, own_rows,
    send_sems, recv_sems, peak_send, peak_recv,
):
    orb = lax.axis_index("orb")
    place = lax.axis_index("wall")
    places = lax.axis_size("wall")
    partners = [{"orb": flipped(orb, q)} for q in range(1, 8)]
    above = {"wall": lax.rem(place + 1, places)}
    below = {"wall": lax.rem(place + places - 1, places)}
    phases = rounds()

    barrier = pltpu.get_barrier_semaphore()
    greeted = [*partners, above, below, *phases[0], *phases[1]]
    for device in greeted:
        pl.semaphore_signal(barrier, inc=1, device_id=device, device_id_type=MESH)

    for b in range(NB):
        blocks[b] = own_ref[:, LN * b : LN * b + LN]
    for q in range(7):
        for g in range(GH):
            outgoing[q, 8 * g : 8 * g + 8, :] = blocks[ghost_ref[q, g]]
    lane_row = lax.broadcasted_iota(jnp.int32, (1, LN), 1)

    def live_block(b):
        block = wall_ref[:, LN * b : LN * b + LN]
        return stack([block[:3], jnp.where(lane_row < count_ref[b], block[3:4], 0.0)])

    edges[0] = live_block(0)
    edges[1] = live_block(WB - 1)

    row = lax.broadcasted_iota(jnp.int32, (LN, 2 * LN), 0)
    lane = lax.broadcasted_iota(jnp.int32, (LN, 2 * LN), 1)
    doubled = jnp.where(row == lane // 32 * 16 + lane % 16, 1.0, 0.0).astype(BF16)

    row = lax.broadcasted_iota(jnp.int32, (LN, LN), 0)
    pick_half = jnp.where((row == 6) | (row == 30) | (row == 46), 1.0, 0.0).astype(BF16)

    def keep_source(j, block):
        geometry, columns = source_tiles(block)
        tile = geometry.astype(BF16).T
        sf[j] = tile
        sh[j] = product(tile, pick_half)
        sc[j] = product(columns, doubled).astype(BF16)

    def build_own(b, carry):
        keep_source(b, blocks[b])
        return carry

    def keep_wall(b, block):
        geometry, columns = wall_tiles(block)
        wf[b] = geometry.astype(BF16).T
        wc[b] = product(columns, doubled).astype(BF16)

    def build_target(b, carry):
        tf[b] = jnp.concatenate([t.astype(BF16) for t in target_tiles(blocks[b])], axis=1)
        return carry

    def diagonal(tile):
        zero = jnp.zeros_like(tile)
        return stack([jnp.concatenate([tile, zero], axis=1), jnp.concatenate([zero, tile], axis=1)])

    lax.fori_loop(0, NB, build_target, 0, unroll=2)
    for b in range(WB):
        keep_wall(b + 1, live_block(b))

    pl.semaphore_wait(barrier, len(greeted))
    edge_copies = [
        send(edges.at[n], edges_in.at[n], send_sems.at[7 + n], recv_sems.at[7 + n], device)
        for n, device in enumerate((below, above))
    ]
    ghost_copies = [
        send(outgoing.at[q], arrived.at[q], send_sems.at[q], recv_sems.at[q], partners[q])
        for q in range(7)
    ]
    for copy in edge_copies:
        copy.start()
    for q in (6, 5, 3, 4, 2, 1, 0):
        ghost_copies[q].start()

    lax.fori_loop(0, NB, build_own, 0, unroll=6)
    for copy in edge_copies:
        copy.wait()
    keep_wall(0, jnp.where(place > 0, edges_in[1], 0.0))
    keep_wall(NW - 1, jnp.where(place < places - 1, edges_in[0], 0.0))

    def gathered(ref, indices):
        return stack([ref[j] for j in indices])

    def paired(ref, indices):
        return jnp.concatenate([gathered(ref, indices[0::2]), gathered(ref, indices[1::2])], axis=1)

    def matrix(cubed, pull):
        terms = two_terms(cubed), two_terms(pull)
        rows = []
        for top in range(0, LN, 16):
            for part in range(2):
                rows.append(jnp.concatenate([t[part][top : top + 16] for t in terms], axis=1))
        return stack(rows)

    group = 4
    tall = KW // 2 * LN

    def wall_geometry(t, wall):
        for n in range(group):
            b = t * group + n
            tiles = paired(wf, [wpair_ref[k, b] for k in range(KW)])
            wall[n * tall : (n + 1) * tall] = product(tiles, diagonal(tf[b, :, :LN]))

    def wall_forces(t, wall):
        for n in range(group):
            b = t * group + n
            total = jnp.zeros((16, 2 * LN), F32)
            for k in range(KW):
                half, side = pl.ds(n * tall + k // 2 * LN, LN), k % 2 * LN
                s, cubed = falloff_of(jnp.maximum(wall[half, side : side + LN], 1e-30))
                total += product(wc[wpair_ref[k, b]], matrix(cubed, cubed * s))
            wsums[b] = total[:8] + total[8:]

    wall_geometry(0, wall0)

    def two_walls(t, carry):
        wall_geometry(2 * t + 1, wall1)
        wall_forces(2 * t, wall0)
        wall_geometry(jnp.minimum(2 * t + 2, NB // group - 1), wall0)
        wall_forces(2 * t + 1, wall1)
        return carry

    lax.fori_loop(0, NB // group // 2, two_walls, 0)

    for q in (0, 1, 2, 4, 3, 5, 6):
        ghost_copies[q].wait()

        def build_ghost(g, carry, q=q):
            keep_source(NB + q * GH + g, arrived[q, pl.ds(pl.multiple_of(g * 8, 8), 8), :])
            return carry

        lax.fori_loop(0, GH, build_ghost, 0, unroll=6)

    def geometry(b, near):
        for n in range(0, K, GROUP):
            indices = [pair_ref[k, b] for k in range(n, n + GROUP)]
            near[pl.ds(n * LN, GROUP * LN), :] = product(gathered(sf, indices), tf[b])

    def forces(b, near):
        total = jnp.zeros((32, 2 * LN), F32)
        half = half_scale * blocks[b, 6:7, :]
        for k in range(K):
            j, tile = pair_ref[k, b], pl.ds(k * LN, LN)
            dist_sq = jnp.maximum(near[tile, :LN], 1e-30)
            s, cubed = falloff_of(dist_sq)
            damp = (dist_sq + eps_scaled) * (sh[j] + half)
            drag = jnp.minimum(near[tile, LN:], 0.0) / damp
            total += product(sc[j], matrix(cubed, cubed * (drag - s)))
        sums[b] = total[:16] + total[16:]

    geometry(0, near0)
    stages = near0, near1

    def some_blocks(t, carry):
        for n in range(UNROLL):
            b = UNROLL * t + n
            geometry(jnp.minimum(b + 1, NB - 1), stages[(n + 1) % 2])
            forces(b, stages[n % 2])
        return carry

    lax.fori_loop(0, NB // UNROLL, some_blocks, 0)

    for b in range(NB):
        own_rows[8 * b : 8 * b + 8, :] = blocks[b]
    state = [own_rows[pl.ds(r, NB, stride=8), :] for r in range(8)]
    y = [(r - center) * inv_support for r in state[:3]]
    v, rho = state[3:6], state[6]
    push = pressure_of(rho) / (rho * rho)
    weigh = [sums[:, r, :LN] for r in range(16)]
    pull = [sums[:, r, LN:] for r in range(16)]
    wweigh = [wsums[:, r, :LN] for r in range(4)]
    wpull = [wsums[:, r, LN:] for r in range(4)]
    square = jnp.zeros((NB, LN), F32)
    forces_out = []
    for c in range(3):
        near = y[c] * weigh[7] - weigh[c]
        wnear = y[c] * wweigh[3] - wweigh[c]
        pressed = push * (near + 2.0 * wnear) + y[c] * weigh[15] - weigh[8 + c]
        pulled = 3.0 * cohesion * near + pull_scale * (y[c] * pull[7] - pull[c])
        pulled += 3.0 * adhesion * wnear - wall_pull_scale * (y[c] * wpull[3] - wpull[c])
        force = (-grad_coeff * support) * pressed - support * pulled
        if c == 2:
            force = force - gravity
        square += force * force
        forces_out.append(force)
    best = jnp.max(jnp.max(square, axis=0, keepdims=True), axis=1, keepdims=True)
    held[0] = jnp.broadcast_to(jnp.sqrt(best), (1, LN))

    def phase_copies(n):
        return [
            send(held.at[n], slots.at[n, t], peak_send.at[n, t], peak_recv.at[n, t], device)
            for t, device in enumerate(phases[n])
        ]

    copies = phase_copies(0)
    for copy in copies:
        copy.start()
    rate = (
        dot3(v, y) * (weigh[7] + wweigh[3])
        - dot3(v, [weigh[c] + wweigh[c] for c in range(3)])
        - dot3(weigh[3:6], y)
        + weigh[6]
    )
    rate_ref[...] = (grad_coeff * support) * rate
    for c in range(3):
        for b in range(NB):
            accel_ref[c : c + 1, LN * b : LN * b + LN] = forces_out[c][b : b + 1]
    for n in range(2):
        best = held[n]
        for t, copy in enumerate(copies):
            copy.wait()
            best = jnp.maximum(best, slots[n, t])
        held[n + 1] = best
        if n == 0:
            copies = phase_copies(1)
            for copy in copies:
                copy.start()
    step_ref[0, 0] = jnp.max(courant * jnp.sqrt(smoothing / (best + 1e-06)))


def per_device(fluid_state, ghost_list, pair_list, wall_state, wall_count, wall_pairs):
    vmem = pl.BlockSpec(memory_space=pltpu.VMEM)
    smem = pl.BlockSpec(memory_space=pltpu.SMEM)
    rates, acceleration, step = pl.pallas_call(
        step_kernel,
        name="step",
        out_shape=(
            jax.ShapeDtypeStruct((NB, LN), F32),
            jax.ShapeDtypeStruct((3, NB * LN), F32),
            jax.ShapeDtypeStruct((1, 1), F32),
        ),
        in_specs=[smem, smem, smem, smem, vmem, vmem],
        out_specs=(vmem, vmem, smem),
        scratch_shapes=[
            pltpu.VMEM((NB, 8, LN), F32),
            pltpu.VMEM((7, GH * 8, LN), F32),
            pltpu.VMEM((7, GH * 8, LN), F32),
            pltpu.VMEM((2, 4, LN), F32),
            pltpu.VMEM((2, 4, LN), F32),
            pltpu.VMEM((3, 1, LN), F32),
            pltpu.VMEM((2, 15, 1, LN), F32),
            pltpu.VMEM((NC, LN, LN), BF16),
            pltpu.VMEM((NC, LN, LN), F32),
            pltpu.VMEM((NC, 32, 2 * LN), BF16),
            pltpu.VMEM((NW, LN, LN), BF16),
            pltpu.VMEM((NW, 16, 2 * LN), BF16),
            pltpu.VMEM((NB, LN, 2 * LN), BF16),
            pltpu.VMEM((NB, 16, 2 * LN), F32),
            pltpu.VMEM((NB, 8, 2 * LN), F32),
        ]
        + [pltpu.VMEM((K * LN, 2 * LN), F32)] * 2
        + [pltpu.VMEM((4 * KW // 2 * LN, 2 * LN), F32)] * 2
        + [
            pltpu.VMEM((NB * 8, LN), F32),
            pltpu.SemaphoreType.DMA((9,)),
            pltpu.SemaphoreType.DMA((9,)),
            pltpu.SemaphoreType.DMA((2, 15)),
            pltpu.SemaphoreType.DMA((2, 15)),
        ],
        compiler_params=pltpu.CompilerParams(collective_id=0, has_side_effects=True),
    )(pair_list.T, wall_pairs.T, ghost_list, wall_count, fluid_state, wall_state)
    return (rates.reshape(-1), acceleration, step.reshape(()))


def solution(mesh):
    return jax.shard_map(
        per_device,
        mesh=mesh,
        in_specs=(
            P(None, ("orb", "wall")),
            P(None, ("orb", "wall")),
            P(("orb", "wall"), None),
            P(None, ("orb", "wall")),
            P(("orb", "wall")),
            P(("orb", "wall"), None),
        ),
        out_specs=(P(("orb", "wall")), P(None, ("orb", "wall")), P()),
        check_vma=False,
    )
```

```python
import jax
import jax.numpy as jnp
from jax import lax
from jax.experimental import pallas as pl
from jax.experimental.pallas import tpu as pltpu
from jax.sharding import PartitionSpec as P

NB = 24
K = 14
KW = 4
GH = 6
WB = 6
EB = 1
NC = NB + 7 * GH
NW = WB + 2 * EB
LN = 128
UNROLL = 4
GROUP = 2

smoothing = 0.1
support = 0.3
kernel_norm = 21.0 / (2.0 * 3.141592653589793 * support**3)
grad_coeff = -20.0 / support**2 * kernel_norm
tait_coeff = 25.0 / 7.0
visc_coeff = 0.05
cohesion = 2000.0
adhesion = 2000.0
gravity = 9.81
courant = 0.25

center = 0.3
inv_support = 1.0 / support
eps_scaled = 0.0001 / support**2
pull_scale = 4.0 * cohesion
wall_pull_scale = 4.0 * adhesion
visc_scaled = visc_coeff * -grad_coeff / support / pull_scale
half_scale = 0.5 / visc_scaled

F32 = jnp.float32
BF16 = jnp.bfloat16


def split(value):
    parts = []
    for _ in range(2):
        high = value.astype(BF16).astype(F32)
        parts.append(high)
        value = value - high
    parts.append(value.astype(BF16).astype(F32))
    return parts


def two_terms(value):
    high = value.astype(BF16)
    return high, (value - high.astype(F32)).astype(BF16)


def pressure_of(density):
    return tait_coeff * (density**7 - 1.0)


def dot3(a, b):
    return a[0] * b[0] + a[1] * b[1] + a[2] * b[2]


def rows_of(block):
    return [block[c : c + 1] for c in range(block.shape[0])]


def stack(rows):
    return jnp.concatenate(rows, axis=0)


CROSS = ((0, 0), (0, 1), (0, 2), (1, 0), (1, 1), (2, 0))


def scaled_rows(block):
    rows = rows_of(block)
    y = [(row - center) * inv_support for row in rows[:3]]
    return y, rows[3:6], rows[6], rows[7]


def wide(groups):
    rows = stack(groups)
    spare = LN - rows.shape[0]
    return stack([rows, jnp.zeros((spare, LN), F32)]) if spare else rows


def source_tiles(block):
    y, v, rho, mass = scaled_rows(block)
    half = half_scale * rho
    one, zero = jnp.ones_like(mass), jnp.zeros_like(mass)
    norm, flow = dot3(y, y), dot3(v, y)
    terms = split(stack(y + v + [half, zero]))
    sums = split(stack([norm, flow, one, one, one, zero, zero, zero]))
    push = pressure_of(rho) / (rho * rho)
    heavy = stack(y + v + [flow, one]) * mass
    pushed = heavy * push
    hh, hl = two_terms(heavy)
    ph, pl_ = two_terms(pushed)
    return wide([terms[j] for j, _ in CROSS] + sums), stack([hh, ph, hl, pl_])


def wall_tiles(block):
    rows = rows_of(block)
    y = [(row - center) * inv_support for row in rows[:3]]
    mass = rows[3]
    one, zero = jnp.ones_like(mass), jnp.zeros_like(mass)
    terms = split(stack(y + [zero] * 5))
    sums = split(stack([dot3(y, y), zero, one, one, one, zero, zero, zero]))
    heavy = stack(y + [one, zero, zero, zero, zero]) * mass
    hh, hl = two_terms(heavy)
    return wide([terms[j] for j, _ in CROSS] + sums), stack([hh, hl])


def target_tiles(block):
    y, v, _, mass = scaled_rows(block)
    one, zero = jnp.ones_like(mass), jnp.zeros_like(mass)
    norm, flow = dot3(y, y), dot3(v, y)
    far = split(stack([-2.0 * c for c in y] + [zero] * 5))
    near = split(stack([-c for c in v] + [-c for c in y] + [zero] * 2))
    far_sum = stack([one, zero] + split(norm) + [zero] * 3)
    near_sum = stack([zero, one] + split(flow) + [zero] * 3)
    return (
        wide([far[i] for _, i in CROSS] + [far_sum] * 3),
        wide([near[i] for _, i in CROSS] + [near_sum] * 3),
    )


def falloff_of(dist_sq):
    s = jnp.maximum(1.0 - dist_sq * lax.rsqrt(dist_sq), 0.0)
    return s, s * s * s


def product(left, right):
    return jnp.dot(left, right, preferred_element_type=F32)


MESH = pl.DeviceIdType.MESH


def flipped(place, pattern):
    partner = place
    for bit in (1, 2, 4):
        if pattern & bit:
            partner = partner + bit - 2 * bit * lax.rem(lax.div(place, bit), 2)
    return partner


def rounds():
    orb = lax.axis_index("orb")
    place = lax.axis_index("wall")
    x, rest = lax.div(orb, 16), lax.rem(orb, 16)
    mine = x * 4 + place
    first = []
    for t in range(1, 16):
        other = lax.rem(mine + t, 16)
        first.append({"orb": lax.div(other, 4) * 16 + rest, "wall": lax.rem(other, 4)})
    second = [{"orb": x * 16 + lax.rem(rest + t, 16), "wall": place} for t in range(1, 16)]
    return first, second


def send(source, target, send_sem, recv_sem, device):
    return pltpu.make_async_remote_copy(
        src_ref=source,
        dst_ref=target,
        send_sem=send_sem,
        recv_sem=recv_sem,
        device_id=device,
        device_id_type=MESH,
    )


def step_kernel(
    pair_in, wpair_in, ghost_in, count_in, own_in, wall_in, rate_out, accel_out, step_ref,
    pair_ref, wpair_ref, ghost_ref, count_ref, own_ref, wall_ref, rate_ref, accel_ref,
    blocks, outgoing, arrived, edges, edges_in, held, slots,
    sf, sh, sc, wf, wc, tf, sums, wsums,
    near0, near1, wall0, wall1, own_rows,
    send_sems, recv_sems, peak_send, peak_recv, load_sems, store_sems,
):
    orb = lax.axis_index("orb")
    place = lax.axis_index("wall")
    places = lax.axis_size("wall")
    partners = [{"orb": flipped(orb, q)} for q in range(1, 8)]
    above = {"wall": lax.rem(place + 1, places)}
    below = {"wall": lax.rem(place + places - 1, places)}
    phases = rounds()

    sources = pair_in, wpair_in, ghost_in, count_in, own_in, wall_in
    targets = pair_ref, wpair_ref, ghost_ref, count_ref, own_ref, wall_ref
    loads = [
        pltpu.make_async_copy(source, target, load_sems.at[n])
        for n, (source, target) in enumerate(zip(sources, targets))
    ]
    for copy in loads:
        copy.start()
    barrier = pltpu.get_barrier_semaphore()
    greeted = [*partners, above, below, *phases[0], *phases[1]]
    for device in greeted:
        pl.semaphore_signal(barrier, inc=1, device_id=device, device_id_type=MESH)

    for copy in loads:
        copy.wait()
    for b in range(NB):
        blocks[b] = own_ref[:, LN * b : LN * b + LN]
    for q in range(7):
        for g in range(GH):
            outgoing[q, 8 * g : 8 * g + 8, :] = blocks[ghost_ref[q, g]]
    lane_row = lax.broadcasted_iota(jnp.int32, (1, LN), 1)

    def live_block(b):
        block = wall_ref[:, LN * b : LN * b + LN]
        return stack([block[:3], jnp.where(lane_row < count_ref[b], block[3:4], 0.0)])

    edges[0] = live_block(0)
    edges[1] = live_block(WB - 1)

    row = lax.broadcasted_iota(jnp.int32, (LN, 2 * LN), 0)
    lane = lax.broadcasted_iota(jnp.int32, (LN, 2 * LN), 1)
    doubled = jnp.where(row == lane // 32 * 16 + lane % 16, 1.0, 0.0).astype(BF16)

    def keep_sources(first, group):
        columns = []
        for n, block in enumerate(group):
            geometry, column = source_tiles(block)
            sf[first + n] = geometry.astype(BF16).T
            sh[first + n] = jnp.broadcast_to(half_scale * block[6:7], (LN, LN)).T
            columns.append(column)
        wide_columns = product(stack(columns), doubled).astype(BF16)
        for n in range(len(group)):
            sc[first + n] = wide_columns[32 * n : 32 * n + 32]

    def build_own(t, carry):
        keep_sources(t * GH, [blocks[t * GH + n] for n in range(GH)])
        return carry

    def keep_wall(b, block):
        geometry, columns = wall_tiles(block)
        wf[b] = geometry.astype(BF16).T
        wc[b] = product(columns, doubled).astype(BF16)

    def build_target(b, carry):
        tf[b] = jnp.concatenate([t.astype(BF16) for t in target_tiles(blocks[b])], axis=1)
        return carry

    def diagonal(tile):
        zero = jnp.zeros_like(tile)
        return stack([jnp.concatenate([tile, zero], axis=1), jnp.concatenate([zero, tile], axis=1)])

    lax.fori_loop(0, NB, build_target, 0, unroll=2)
    lax.fori_loop(0, NB // GH, build_own, 0)
    for b in range(WB):
        keep_wall(b + 1, live_block(b))

    pl.semaphore_wait(barrier, len(greeted))
    edge_copies = [
        send(edges.at[n], edges_in.at[n], send_sems.at[7 + n], recv_sems.at[7 + n], device)
        for n, device in enumerate((below, above))
    ]
    ghost_copies = [
        send(outgoing.at[q], arrived.at[q], send_sems.at[q], recv_sems.at[q], partners[q])
        for q in range(7)
    ]
    for copy in edge_copies:
        copy.start()
    for q in (6, 5, 3, 4, 2, 1, 0):
        ghost_copies[q].start()

    for copy in edge_copies:
        copy.wait()
    keep_wall(0, jnp.where(place > 0, edges_in[1], 0.0))
    keep_wall(NW - 1, jnp.where(place < places - 1, edges_in[0], 0.0))

    def gathered(ref, indices):
        return stack([ref[j] for j in indices])

    def paired(ref, indices):
        return jnp.concatenate([gathered(ref, indices[0::2]), gathered(ref, indices[1::2])], axis=1)

    def matrix(cubed, pull):
        terms = two_terms(cubed), two_terms(pull)
        rows = []
        for top in range(0, LN, 16):
            for part in range(2):
                rows.append(jnp.concatenate([t[part][top : top + 16] for t in terms], axis=1))
        return stack(rows)

    group = 4
    tall = KW // 2 * LN

    def wall_geometry(t, wall):
        for n in range(group):
            b = t * group + n
            tiles = paired(wf, [wpair_ref[k, b] for k in range(KW)])
            wall[n * tall : (n + 1) * tall] = product(tiles, diagonal(tf[b, :, :LN]))

    def wall_forces(t, wall):
        for n in range(group):
            b = t * group + n
            total = jnp.zeros((16, 2 * LN), F32)
            for k in range(KW):
                half, side = pl.ds(n * tall + k // 2 * LN, LN), k % 2 * LN
                s, cubed = falloff_of(jnp.maximum(wall[half, side : side + LN], 1e-30))
                total += product(wc[wpair_ref[k, b]], matrix(cubed, cubed * s))
            wsums[b] = total[:8] + total[8:]

    wall_geometry(0, wall0)

    def two_walls(t, carry):
        wall_geometry(2 * t + 1, wall1)
        wall_forces(2 * t, wall0)
        wall_geometry(jnp.minimum(2 * t + 2, NB // group - 1), wall0)
        wall_forces(2 * t + 1, wall1)
        return carry

    lax.fori_loop(0, NB // group // 2, two_walls, 0)

    for q in (0, 1, 2, 4, 3, 5, 6):
        ghost_copies[q].wait()
        keep_sources(NB + q * GH, [arrived[q, 8 * g : 8 * g + 8, :] for g in range(GH)])

    def geometry(b, near):
        for n in range(0, K, GROUP):
            indices = [pair_ref[k, b] for k in range(n, n + GROUP)]
            near[pl.ds(n * LN, GROUP * LN), :] = product(gathered(sf, indices), tf[b])

    def forces(b, near):
        total = jnp.zeros((32, 2 * LN), F32)
        half = half_scale * blocks[b, 6:7, :]
        for k in range(K):
            j, tile = pair_ref[k, b], pl.ds(k * LN, LN)
            dist_sq = jnp.maximum(near[tile, :LN], 1e-30)
            s, cubed = falloff_of(dist_sq)
            damp = (dist_sq + eps_scaled) * (sh[j] + half)
            drag = jnp.minimum(near[tile, LN:], 0.0) / damp
            total += product(sc[j], matrix(cubed, cubed * (drag - s)))
        sums[b] = total[:16] + total[16:]

    geometry(0, near0)
    stages = near0, near1

    def some_blocks(t, carry):
        for n in range(UNROLL):
            b = UNROLL * t + n
            geometry(jnp.minimum(b + 1, NB - 1), stages[(n + 1) % 2])
            forces(b, stages[n % 2])
        return carry

    lax.fori_loop(0, NB // UNROLL, some_blocks, 0)

    for b in range(NB):
        own_rows[8 * b : 8 * b + 8, :] = blocks[b]
    state = [own_rows[pl.ds(r, NB, stride=8), :] for r in range(8)]
    y = [(r - center) * inv_support for r in state[:3]]
    v, rho = state[3:6], state[6]
    push = pressure_of(rho) / (rho * rho)
    weigh = [sums[:, r, :LN] for r in range(16)]
    pull = [sums[:, r, LN:] for r in range(16)]
    wweigh = [wsums[:, r, :LN] for r in range(4)]
    wpull = [wsums[:, r, LN:] for r in range(4)]
    square = jnp.zeros((NB, LN), F32)
    forces_out = []
    for c in range(3):
        near = y[c] * weigh[7] - weigh[c]
        wnear = y[c] * wweigh[3] - wweigh[c]
        pressed = push * (near + 2.0 * wnear) + y[c] * weigh[15] - weigh[8 + c]
        pulled = 3.0 * cohesion * near + pull_scale * (y[c] * pull[7] - pull[c])
        pulled += 3.0 * adhesion * wnear - wall_pull_scale * (y[c] * wpull[3] - wpull[c])
        force = (-grad_coeff * support) * pressed - support * pulled
        if c == 2:
            force = force - gravity
        square += force * force
        forces_out.append(force)
    best = jnp.max(jnp.max(square, axis=0, keepdims=True), axis=1, keepdims=True)
    held[0] = jnp.broadcast_to(jnp.sqrt(best), (1, LN))

    def phase_copies(n):
        return [
            send(held.at[n], slots.at[n, t], peak_send.at[n, t], peak_recv.at[n, t], device)
            for t, device in enumerate(phases[n])
        ]

    copies = phase_copies(0)
    for copy in copies:
        copy.start()
    rate = (
        dot3(v, y) * (weigh[7] + wweigh[3])
        - dot3(v, [weigh[c] + wweigh[c] for c in range(3)])
        - dot3(weigh[3:6], y)
        + weigh[6]
    )
    rate_ref[...] = (grad_coeff * support) * rate
    for c in range(3):
        for b in range(NB):
            accel_ref[c : c + 1, LN * b : LN * b + LN] = forces_out[c][b : b + 1]
    stores = [
        pltpu.make_async_copy(rate_ref, rate_out, store_sems.at[0]),
        pltpu.make_async_copy(accel_ref, accel_out, store_sems.at[1]),
    ]
    for copy in stores:
        copy.start()
    for n in range(2):
        best = held[n]
        for t, copy in enumerate(copies):
            copy.wait()
            best = jnp.maximum(best, slots[n, t])
        held[n + 1] = best
        if n == 0:
            copies = phase_copies(1)
            for copy in copies:
                copy.start()
    step_ref[0, 0] = jnp.max(courant * jnp.sqrt(smoothing / (best + 1e-06)))
    for copy in stores:
        copy.wait()


def handed_on(rates, acceleration):
    def kernel(rate_ref, accel_ref, rate_out, accel_out):
        rate_out[...] = rate_ref[...]
        accel_out[...] = accel_ref[...]

    vmem = pl.BlockSpec(memory_space=pltpu.VMEM)
    shapes = jax.ShapeDtypeStruct((NB, LN), F32), jax.ShapeDtypeStruct((3, NB * LN), F32)
    return pl.pallas_call(
        kernel, name="handed_on", out_shape=shapes, in_specs=[vmem, vmem], out_specs=(vmem, vmem)
    )(rates, acceleration)


def per_device(fluid_state, ghost_list, pair_list, wall_state, wall_count, wall_pairs):
    anywhere = pl.BlockSpec(memory_space=pl.ANY)
    smem = pl.BlockSpec(memory_space=pltpu.SMEM)
    rates, acceleration, step = pl.pallas_call(
        step_kernel,
        name="step",
        out_shape=(
            jax.ShapeDtypeStruct((NB, LN), F32),
            jax.ShapeDtypeStruct((3, NB * LN), F32),
            jax.ShapeDtypeStruct((1, 1), F32),
        ),
        in_specs=[anywhere] * 6,
        out_specs=(anywhere, anywhere, smem),
        scratch_shapes=[
            pltpu.SMEM((K, NB), jnp.int32),
            pltpu.SMEM((KW, NB), jnp.int32),
            pltpu.SMEM((7, GH), jnp.int32),
            pltpu.SMEM((WB,), jnp.int32),
            pltpu.VMEM((8, NB * LN), F32),
            pltpu.VMEM((4, WB * LN), F32),
            pltpu.VMEM((NB, LN), F32),
            pltpu.VMEM((3, NB * LN), F32),
            pltpu.VMEM((NB, 8, LN), F32),
            pltpu.VMEM((7, GH * 8, LN), F32),
            pltpu.VMEM((7, GH * 8, LN), F32),
            pltpu.VMEM((2, 4, LN), F32),
            pltpu.VMEM((2, 4, LN), F32),
            pltpu.VMEM((3, 1, LN), F32),
            pltpu.VMEM((2, 15, 1, LN), F32),
            pltpu.VMEM((NC, LN, LN), BF16),
            pltpu.VMEM((NC, LN, LN), F32),
            pltpu.VMEM((NC, 32, 2 * LN), BF16),
            pltpu.VMEM((NW, LN, LN), BF16),
            pltpu.VMEM((NW, 16, 2 * LN), BF16),
            pltpu.VMEM((NB, LN, 2 * LN), BF16),
            pltpu.VMEM((NB, 16, 2 * LN), F32),
            pltpu.VMEM((NB, 8, 2 * LN), F32),
        ]
        + [pltpu.VMEM((K * LN, 2 * LN), F32)] * 2
        + [pltpu.VMEM((4 * KW // 2 * LN, 2 * LN), F32)] * 2
        + [
            pltpu.VMEM((NB * 8, LN), F32),
            pltpu.SemaphoreType.DMA((9,)),
            pltpu.SemaphoreType.DMA((9,)),
            pltpu.SemaphoreType.DMA((2, 15)),
            pltpu.SemaphoreType.DMA((2, 15)),
            pltpu.SemaphoreType.DMA((6,)),
            pltpu.SemaphoreType.DMA((2,)),
        ],
        compiler_params=pltpu.CompilerParams(collective_id=0, has_side_effects=True),
    )(pair_list.T, wall_pairs.T, ghost_list, wall_count, fluid_state, wall_state)
    rates, acceleration = handed_on(rates, acceleration)
    return (rates.reshape(-1), acceleration, step.reshape(()))


def solution(mesh):
    return jax.shard_map(
        per_device,
        mesh=mesh,
        in_specs=(
            P(None, ("orb", "wall")),
            P(None, ("orb", "wall")),
            P(("orb", "wall"), None),
            P(None, ("orb", "wall")),
            P(("orb", "wall")),
            P(("orb", "wall"), None),
        ),
        out_specs=(P(("orb", "wall")), P(None, ("orb", "wall")), P()),
        check_vma=False,
    )
```

```python
import jax
import jax.numpy as jnp
from jax import lax
from jax.experimental import pallas as pl
from jax.experimental.pallas import tpu as pltpu
from jax.sharding import PartitionSpec as P

NB = 24
K = 14
KW = 4
GH = 6
WB = 6
EB = 1
NC = NB + 7 * GH
NW = WB + 2 * EB
LN = 128
UNROLL = 4
WALL_LAG = 12
GROUP = 2

smoothing = 0.1
support = 0.3
kernel_norm = 21.0 / (2.0 * 3.141592653589793 * support**3)
grad_coeff = -20.0 / support**2 * kernel_norm
tait_coeff = 25.0 / 7.0
visc_coeff = 0.05
cohesion = 2000.0
adhesion = 2000.0
gravity = 9.81
courant = 0.25

center = 0.3
inv_support = 1.0 / support
eps_scaled = 0.0001 / support**2
pull_scale = 4.0 * cohesion
wall_pull_scale = 4.0 * adhesion
visc_scaled = visc_coeff * -grad_coeff / support / pull_scale
half_scale = 0.5 / visc_scaled

F32 = jnp.float32
BF16 = jnp.bfloat16


def split(value):
    parts = []
    for _ in range(2):
        high = value.astype(BF16).astype(F32)
        parts.append(high)
        value = value - high
    parts.append(value.astype(BF16).astype(F32))
    return parts


def two_terms(value):
    high = value.astype(BF16)
    return high, (value - high.astype(F32)).astype(BF16)


def pressure_of(density):
    return tait_coeff * (density**7 - 1.0)


def dot3(a, b):
    return a[0] * b[0] + a[1] * b[1] + a[2] * b[2]


def rows_of(block):
    return [block[c : c + 1] for c in range(block.shape[0])]


def stack(rows):
    return jnp.concatenate(rows, axis=0)


CROSS = ((0, 0), (0, 1), (0, 2), (1, 0), (1, 1), (2, 0))


def scaled_rows(block):
    rows = rows_of(block)
    y = [(row - center) * inv_support for row in rows[:3]]
    return y, rows[3:6], rows[6], rows[7]


def wide(groups):
    rows = stack(groups)
    spare = LN - rows.shape[0]
    return stack([rows, jnp.zeros((spare, LN), F32)]) if spare else rows


def source_tiles(block):
    y, v, rho, mass = scaled_rows(block)
    half = half_scale * rho
    one, zero = jnp.ones_like(mass), jnp.zeros_like(mass)
    norm, flow = dot3(y, y), dot3(v, y)
    terms = split(stack(y + v + [half, zero]))
    sums = split(stack([norm, flow, one, one, one, zero, zero, zero]))
    push = pressure_of(rho) / (rho * rho)
    heavy = stack(y + v + [flow, one]) * mass
    pushed = heavy * push
    hh, hl = two_terms(heavy)
    ph, pl_ = two_terms(pushed)
    return wide([terms[j] for j, _ in CROSS] + sums), stack([hh, ph, hl, pl_])


def wall_tiles(block):
    rows = rows_of(block)
    y = [(row - center) * inv_support for row in rows[:3]]
    mass = rows[3]
    one, zero = jnp.ones_like(mass), jnp.zeros_like(mass)
    terms = split(stack(y + [zero] * 5))
    sums = split(stack([dot3(y, y), zero, one, one, one, zero, zero, zero]))
    heavy = stack(y + [one, zero, zero, zero, zero]) * mass
    hh, hl = two_terms(heavy)
    return wide([terms[j] for j, _ in CROSS] + sums), stack([hh, hl])


def target_tiles(block):
    y, v, _, mass = scaled_rows(block)
    one, zero = jnp.ones_like(mass), jnp.zeros_like(mass)
    norm, flow = dot3(y, y), dot3(v, y)
    far = split(stack([-2.0 * c for c in y] + [zero] * 5))
    near = split(stack([-c for c in v] + [-c for c in y] + [zero] * 2))
    far_sum = stack([one, zero] + split(norm) + [zero] * 3)
    near_sum = stack([zero, one] + split(flow) + [zero] * 3)
    return (
        wide([far[i] for _, i in CROSS] + [far_sum] * 3),
        wide([near[i] for _, i in CROSS] + [near_sum] * 3),
    )


def falloff_of(dist_sq):
    s = jnp.maximum(1.0 - dist_sq * lax.rsqrt(dist_sq), 0.0)
    return s, s * s * s


def product(left, right):
    return jnp.dot(left, right, preferred_element_type=F32)


MESH = pl.DeviceIdType.MESH


def flipped(place, pattern):
    partner = place
    for bit in (1, 2, 4):
        if pattern & bit:
            partner = partner + bit - 2 * bit * lax.rem(lax.div(place, bit), 2)
    return partner


def rounds():
    orb = lax.axis_index("orb")
    place = lax.axis_index("wall")
    x, rest = lax.div(orb, 16), lax.rem(orb, 16)
    mine = x * 4 + place
    first = []
    for t in range(1, 16):
        other = lax.rem(mine + t, 16)
        first.append({"orb": lax.div(other, 4) * 16 + rest, "wall": lax.rem(other, 4)})
    second = [{"orb": x * 16 + lax.rem(rest + t, 16), "wall": place} for t in range(1, 16)]
    return first, second


def send(source, target, send_sem, recv_sem, device):
    return pltpu.make_async_remote_copy(
        src_ref=source,
        dst_ref=target,
        send_sem=send_sem,
        recv_sem=recv_sem,
        device_id=device,
        device_id_type=MESH,
    )


def step_kernel(
    pair_in, wpair_in, ghost_in, count_in, own_in, wall_in, rate_out, accel_out, step_ref,
    pair_ref, wpair_ref, ghost_ref, count_ref, own_ref, wall_ref, rate_ref, accel_ref,
    blocks, outgoing, arrived, edges, edges_in, held, slots,
    sf, sh, sc, wf, wc, tf, sums, wsums,
    near0, near1, wall0, wall1, own_rows,
    send_sems, recv_sems, peak_send, peak_recv, load_sems, store_sems,
):
    orb = lax.axis_index("orb")
    place = lax.axis_index("wall")
    places = lax.axis_size("wall")
    partners = [{"orb": flipped(orb, q)} for q in range(1, 8)]
    above = {"wall": lax.rem(place + 1, places)}
    below = {"wall": lax.rem(place + places - 1, places)}
    phases = rounds()

    sources = pair_in, wpair_in, ghost_in, count_in, own_in, wall_in
    targets = pair_ref, wpair_ref, ghost_ref, count_ref, own_ref, wall_ref
    loads = [
        pltpu.make_async_copy(source, target, load_sems.at[n])
        for n, (source, target) in enumerate(zip(sources, targets))
    ]
    for copy in loads:
        copy.start()
    barrier = pltpu.get_barrier_semaphore()
    far_first = sorted(range(15), key=lambda t: abs(t - 7))
    greeted = [phases[n][t] for t in far_first for n in range(2)] + [*partners, above, below]
    for device in greeted:
        pl.semaphore_signal(barrier, inc=1, device_id=device, device_id_type=MESH)

    for copy in loads:
        copy.wait()
    for b in range(NB):
        blocks[b] = own_ref[:, LN * b : LN * b + LN]
    for q in range(7):
        for g in range(GH):
            outgoing[q, 8 * g : 8 * g + 8, :] = blocks[ghost_ref[q, g]]
    lane_row = lax.broadcasted_iota(jnp.int32, (1, LN), 1)

    def live_block(b):
        block = wall_ref[:, LN * b : LN * b + LN]
        return stack([block[:3], jnp.where(lane_row < count_ref[b], block[3:4], 0.0)])

    edges[0] = live_block(0)
    edges[1] = live_block(WB - 1)

    row = lax.broadcasted_iota(jnp.int32, (LN, 2 * LN), 0)
    lane = lax.broadcasted_iota(jnp.int32, (LN, 2 * LN), 1)
    doubled = jnp.where(row == lane // 32 * 16 + lane % 16, 1.0, 0.0).astype(BF16)

    def keep_sources(first, group):
        columns = []
        for n, block in enumerate(group):
            geometry, column = source_tiles(block)
            sf[first + n] = geometry.astype(BF16).T
            sh[first + n] = jnp.broadcast_to(half_scale * block[6:7], (LN, LN)).T
            columns.append(column)
        wide_columns = product(stack(columns), doubled).astype(BF16)
        for n in range(len(group)):
            sc[first + n] = wide_columns[32 * n : 32 * n + 32]

    def build_own(t, carry):
        keep_sources(t * GH, [blocks[t * GH + n] for n in range(GH)])
        return carry

    def keep_wall(b, block):
        geometry, columns = wall_tiles(block)
        wf[b] = geometry.astype(BF16).T
        wc[b] = product(columns, doubled).astype(BF16)

    def build_target(b, carry):
        tf[b] = jnp.concatenate([t.astype(BF16) for t in target_tiles(blocks[b])], axis=1)
        return carry

    def diagonal(tile):
        zero = jnp.zeros_like(tile)
        return stack([jnp.concatenate([tile, zero], axis=1), jnp.concatenate([zero, tile], axis=1)])

    lax.fori_loop(0, NB, build_target, 0, unroll=2)
    lax.fori_loop(0, NB // GH, build_own, 0)
    for b in range(WB):
        keep_wall(b + 1, live_block(b))

    pl.semaphore_wait(barrier, len(greeted))
    edge_copies = [
        send(edges.at[n], edges_in.at[n], send_sems.at[7 + n], recv_sems.at[7 + n], device)
        for n, device in enumerate((below, above))
    ]
    ghost_copies = [
        send(outgoing.at[q], arrived.at[q], send_sems.at[q], recv_sems.at[q], partners[q])
        for q in range(7)
    ]
    for copy in edge_copies:
        copy.start()
    for q in (6, 5, 3, 4, 2, 1, 0):
        ghost_copies[q].start()

    for copy in edge_copies:
        copy.wait()
    keep_wall(0, jnp.where(place > 0, edges_in[1], 0.0))
    keep_wall(NW - 1, jnp.where(place < places - 1, edges_in[0], 0.0))

    def gathered(ref, indices):
        return stack([ref[j] for j in indices])

    def paired(ref, indices):
        return jnp.concatenate([gathered(ref, indices[0::2]), gathered(ref, indices[1::2])], axis=1)

    def matrix(cubed, pull):
        terms = two_terms(cubed), two_terms(pull)
        rows = []
        for top in range(0, LN, 16):
            for part in range(2):
                rows.append(jnp.concatenate([t[part][top : top + 16] for t in terms], axis=1))
        return stack(rows)

    group = 4
    tall = KW // 2 * LN

    def wall_geometry(t, wall):
        for n in range(group):
            b = t * group + n
            tiles = paired(wf, [wpair_ref[k, b] for k in range(KW)])
            wall[n * tall : (n + 1) * tall] = product(tiles, diagonal(tf[b, :, :LN]))

    def wall_forces(t, wall, at):
        past = []
        for n in range(group):
            b = t * group + n
            total = jnp.zeros((16, 2 * LN), F32)
            for k in range(KW):
                if len(past) >= WALL_LAG:
                    row = pl.multiple_of(group * tall + 16 * at, 16)
                    wall[pl.ds(row, 16), :] = past[len(past) - WALL_LAG]
                half, side = pl.ds(n * tall + k // 2 * LN, LN), k % 2 * LN
                s, cubed = falloff_of(jnp.maximum(wall[half, side : side + LN], 1e-30))
                total += product(wc[wpair_ref[k, b]], matrix(cubed, cubed * s))
                past.append(total)
            wsums[b] = total[:8] + total[8:]

    wall_geometry(0, wall0)

    def two_walls(t, carry):
        wall_geometry(2 * t + 1, wall1)
        at = lax.div(t, NB)
        wall_forces(2 * t, wall0, at)
        wall_geometry(jnp.minimum(2 * t + 2, NB // group - 1), wall0)
        wall_forces(2 * t + 1, wall1, at)
        return carry

    lax.fori_loop(0, NB // group // 2, two_walls, 0)

    for q in (0, 1, 2, 4, 3, 5, 6):
        ghost_copies[q].wait()
        keep_sources(NB + q * GH, [arrived[q, 8 * g : 8 * g + 8, :] for g in range(GH)])

    def geometry(b, near):
        for n in range(0, K, GROUP):
            indices = [pair_ref[k, b] for k in range(n, n + GROUP)]
            near[pl.ds(n * LN, GROUP * LN), :] = product(gathered(sf, indices), tf[b])

    def forces(b, near):
        total = jnp.zeros((32, 2 * LN), F32)
        half = half_scale * blocks[b, 6:7, :]
        for k in range(K):
            j, tile = pair_ref[k, b], pl.ds(k * LN, LN)
            dist_sq = jnp.maximum(near[tile, :LN], 1e-30)
            s, cubed = falloff_of(dist_sq)
            damp = (dist_sq + eps_scaled) * (sh[j] + half)
            drag = jnp.minimum(near[tile, LN:], 0.0) / damp
            total += product(sc[j], matrix(cubed, cubed * (drag - s)))
        sums[b] = total[:16] + total[16:]

    geometry(0, near0)
    stages = near0, near1

    def some_blocks(t, carry):
        for n in range(UNROLL):
            b = UNROLL * t + n
            geometry(jnp.minimum(b + 1, NB - 1), stages[(n + 1) % 2])
            forces(b, stages[n % 2])
        return carry

    lax.fori_loop(0, NB // UNROLL, some_blocks, 0)

    for b in range(NB):
        own_rows[8 * b : 8 * b + 8, :] = blocks[b]
    state = [own_rows[pl.ds(r, NB, stride=8), :] for r in range(8)]
    y = [(r - center) * inv_support for r in state[:3]]
    v, rho = state[3:6], state[6]
    push = pressure_of(rho) / (rho * rho)
    weigh = [sums[:, r, :LN] for r in range(16)]
    pull = [sums[:, r, LN:] for r in range(16)]
    wweigh = [wsums[:, r, :LN] for r in range(4)]
    wpull = [wsums[:, r, LN:] for r in range(4)]
    square = jnp.zeros((NB, LN), F32)
    forces_out = []
    for c in range(3):
        near = y[c] * weigh[7] - weigh[c]
        wnear = y[c] * wweigh[3] - wweigh[c]
        pressed = push * (near + 2.0 * wnear) + y[c] * weigh[15] - weigh[8 + c]
        pulled = 3.0 * cohesion * near + pull_scale * (y[c] * pull[7] - pull[c])
        pulled += 3.0 * adhesion * wnear - wall_pull_scale * (y[c] * wpull[3] - wpull[c])
        force = (-grad_coeff * support) * pressed - support * pulled
        if c == 2:
            force = force - gravity
        square += force * force
        forces_out.append(force)
    best = jnp.max(jnp.max(square, axis=0, keepdims=True), axis=1, keepdims=True)
    held[0] = jnp.broadcast_to(jnp.sqrt(best), (1, LN))

    def phase_copies(n):
        return [
            send(held.at[n], slots.at[n, t], peak_send.at[n, t], peak_recv.at[n, t], device)
            for t, device in enumerate(phases[n])
        ]

    copies = phase_copies(0)
    for copy in copies:
        copy.start()
    rate = (
        dot3(v, y) * (weigh[7] + wweigh[3])
        - dot3(v, [weigh[c] + wweigh[c] for c in range(3)])
        - dot3(weigh[3:6], y)
        + weigh[6]
    )
    rate_ref[...] = (grad_coeff * support) * rate
    for c in range(3):
        for b in range(NB):
            accel_ref[c : c + 1, LN * b : LN * b + LN] = forces_out[c][b : b + 1]
    stores = [
        pltpu.make_async_copy(rate_ref, rate_out, store_sems.at[0]),
        pltpu.make_async_copy(accel_ref, accel_out, store_sems.at[1]),
    ]
    for copy in stores:
        copy.start()
    for n in range(2):
        best = held[n]
        for t, copy in enumerate(copies):
            copy.wait()
            best = jnp.maximum(best, slots[n, t])
        held[n + 1] = best
        if n == 0:
            copies = phase_copies(1)
            for copy in copies:
                copy.start()
    step_ref[0, 0] = jnp.max(courant * jnp.sqrt(smoothing / (best + 1e-06)))
    for copy in stores:
        copy.wait()


def handed_on(rates, acceleration):
    def kernel(rate_ref, accel_ref, rate_out, accel_out):
        rate_out[...] = rate_ref[...]
        accel_out[...] = accel_ref[...]

    vmem = pl.BlockSpec(memory_space=pltpu.VMEM)
    shapes = jax.ShapeDtypeStruct((NB, LN), F32), jax.ShapeDtypeStruct((3, NB * LN), F32)
    return pl.pallas_call(
        kernel, name="handed_on", out_shape=shapes, in_specs=[vmem, vmem], out_specs=(vmem, vmem)
    )(rates, acceleration)


def per_device(fluid_state, ghost_list, pair_list, wall_state, wall_count, wall_pairs):
    anywhere = pl.BlockSpec(memory_space=pl.ANY)
    smem = pl.BlockSpec(memory_space=pltpu.SMEM)
    rates, acceleration, step = pl.pallas_call(
        step_kernel,
        name="step",
        out_shape=(
            jax.ShapeDtypeStruct((NB, LN), F32),
            jax.ShapeDtypeStruct((3, NB * LN), F32),
            jax.ShapeDtypeStruct((1, 1), F32),
        ),
        in_specs=[anywhere] * 6,
        out_specs=(anywhere, anywhere, smem),
        scratch_shapes=[
            pltpu.SMEM((K, NB), jnp.int32),
            pltpu.SMEM((KW, NB), jnp.int32),
            pltpu.SMEM((7, GH), jnp.int32),
            pltpu.SMEM((WB,), jnp.int32),
            pltpu.VMEM((8, NB * LN), F32),
            pltpu.VMEM((4, WB * LN), F32),
            pltpu.VMEM((NB, LN), F32),
            pltpu.VMEM((3, NB * LN), F32),
            pltpu.VMEM((NB, 8, LN), F32),
            pltpu.VMEM((7, GH * 8, LN), F32),
            pltpu.VMEM((7, GH * 8, LN), F32),
            pltpu.VMEM((2, 4, LN), F32),
            pltpu.VMEM((2, 4, LN), F32),
            pltpu.VMEM((3, 1, LN), F32),
            pltpu.VMEM((2, 15, 1, LN), F32),
            pltpu.VMEM((NC, LN, LN), BF16),
            pltpu.VMEM((NC, LN, LN), F32),
            pltpu.VMEM((NC, 32, 2 * LN), BF16),
            pltpu.VMEM((NW, LN, LN), BF16),
            pltpu.VMEM((NW, 16, 2 * LN), BF16),
            pltpu.VMEM((NB, LN, 2 * LN), BF16),
            pltpu.VMEM((NB, 16, 2 * LN), F32),
            pltpu.VMEM((NB, 8, 2 * LN), F32),
        ]
        + [pltpu.VMEM((K * LN, 2 * LN), F32)] * 2
        + [pltpu.VMEM((4 * KW // 2 * LN + 32, 2 * LN), F32)] * 2
        + [
            pltpu.VMEM((NB * 8, LN), F32),
            pltpu.SemaphoreType.DMA((9,)),
            pltpu.SemaphoreType.DMA((9,)),
            pltpu.SemaphoreType.DMA((2, 15)),
            pltpu.SemaphoreType.DMA((2, 15)),
            pltpu.SemaphoreType.DMA((6,)),
            pltpu.SemaphoreType.DMA((2,)),
        ],
        compiler_params=pltpu.CompilerParams(collective_id=0, has_side_effects=True),
    )(pair_list.T, wall_pairs.T, ghost_list, wall_count, fluid_state, wall_state)
    rates, acceleration = handed_on(rates, acceleration)
    return (rates.reshape(-1), acceleration, step.reshape(()))


def solution(mesh):
    return jax.shard_map(
        per_device,
        mesh=mesh,
        in_specs=(
            P(None, ("orb", "wall")),
            P(None, ("orb", "wall")),
            P(("orb", "wall"), None),
            P(None, ("orb", "wall")),
            P(("orb", "wall")),
            P(("orb", "wall"), None),
        ),
        out_specs=(P(("orb", "wall")), P(None, ("orb", "wall")), P()),
        check_vma=False,
    )
```

```python
import jax
import jax.numpy as jnp
from jax import lax
from jax.experimental import pallas as pl
from jax.experimental.pallas import tpu as pltpu
from jax.sharding import PartitionSpec as P

NB = 24
K = 14
KW = 4
GH = 6
WB = 6
EB = 1
NC = NB + 7 * GH
NW = WB + 2 * EB
LN = 128
UNROLL = 4
WALL_LAG = 12
GROUP = 2

smoothing = 0.1
support = 0.3
kernel_norm = 21.0 / (2.0 * 3.141592653589793 * support**3)
grad_coeff = -20.0 / support**2 * kernel_norm
tait_coeff = 25.0 / 7.0
visc_coeff = 0.05
cohesion = 2000.0
adhesion = 2000.0
gravity = 9.81
courant = 0.25

center = 0.3
inv_support = 1.0 / support
eps_scaled = 0.0001 / support**2
pull_scale = 4.0 * cohesion
wall_pull_scale = 4.0 * adhesion
visc_scaled = visc_coeff * -grad_coeff / support / pull_scale
half_scale = 0.5 / visc_scaled

F32 = jnp.float32
BF16 = jnp.bfloat16


def split(value):
    parts = []
    for _ in range(2):
        high = value.astype(BF16).astype(F32)
        parts.append(high)
        value = value - high
    parts.append(value.astype(BF16).astype(F32))
    return parts


def two_terms(value):
    high = value.astype(BF16)
    return high, (value - high.astype(F32)).astype(BF16)


def pressure_of(density):
    return tait_coeff * (density**7 - 1.0)


def dot3(a, b):
    return a[0] * b[0] + a[1] * b[1] + a[2] * b[2]


def rows_of(block):
    return [block[c : c + 1] for c in range(block.shape[0])]


def stack(rows):
    return jnp.concatenate(rows, axis=0)


CROSS = ((0, 0), (0, 1), (0, 2), (1, 0), (1, 1), (2, 0))


def scaled_rows(block):
    rows = rows_of(block)
    y = [(row - center) * inv_support for row in rows[:3]]
    return y, rows[3:6], rows[6], rows[7]


def wide(groups):
    rows = stack(groups)
    spare = LN - rows.shape[0]
    return stack([rows, jnp.zeros((spare, LN), F32)]) if spare else rows


def source_tiles(block):
    y, v, rho, mass = scaled_rows(block)
    half = half_scale * rho
    one, zero = jnp.ones_like(mass), jnp.zeros_like(mass)
    norm, flow = dot3(y, y), dot3(v, y)
    terms = split(stack(y + v + [half, zero]))
    sums = split(stack([norm, flow, one, one, one, zero, zero, zero]))
    push = pressure_of(rho) / (rho * rho)
    heavy = stack(y + v + [flow, one]) * mass
    pushed = heavy * push
    hh, hl = two_terms(heavy)
    ph, pl_ = two_terms(pushed)
    return wide([terms[j] for j, _ in CROSS] + sums), stack([hh, ph, hl, pl_])


def wall_tiles(block):
    rows = rows_of(block)
    y = [(row - center) * inv_support for row in rows[:3]]
    mass = rows[3]
    one, zero = jnp.ones_like(mass), jnp.zeros_like(mass)
    terms = split(stack(y + [zero] * 5))
    sums = split(stack([dot3(y, y), zero, one, one, one, zero, zero, zero]))
    heavy = stack(y + [one, zero, zero, zero, zero]) * mass
    hh, hl = two_terms(heavy)
    return wide([terms[j] for j, _ in CROSS] + sums), stack([hh, hl])


def target_tiles(block):
    y, v, _, mass = scaled_rows(block)
    one, zero = jnp.ones_like(mass), jnp.zeros_like(mass)
    norm, flow = dot3(y, y), dot3(v, y)
    far = split(stack([-2.0 * c for c in y] + [zero] * 5))
    near = split(stack([-c for c in v] + [-c for c in y] + [zero] * 2))
    far_sum = stack([one, zero] + split(norm) + [zero] * 3)
    near_sum = stack([zero, one] + split(flow) + [zero] * 3)
    return (
        wide([far[i] for _, i in CROSS] + [far_sum] * 3),
        wide([near[i] for _, i in CROSS] + [near_sum] * 3),
    )


def falloff_of(dist_sq):
    s = jnp.maximum(1.0 - dist_sq * lax.rsqrt(dist_sq), 0.0)
    return s, s * s * s


def product(left, right):
    return jnp.dot(left, right, preferred_element_type=F32)


MESH = pl.DeviceIdType.MESH


def flipped(place, pattern):
    partner = place
    for bit in (1, 2, 4):
        if pattern & bit:
            partner = partner + bit - 2 * bit * lax.rem(lax.div(place, bit), 2)
    return partner


def farthest_first(long, short):
    steps = [(i, j) for i in range(long) for j in range(short) if i or j]
    return sorted(steps, key=lambda step: -min(step[0], long - step[0]) - min(step[1], short - step[1]))


def rounds():
    orb = lax.axis_index("orb")
    place = lax.axis_index("wall")
    x, rest = lax.div(orb, 16), lax.rem(orb, 16)
    z, core = lax.div(rest, 2), lax.rem(rest, 2)
    first = [
        {"orb": lax.rem(x + i, 4) * 16 + rest, "wall": lax.rem(place + j, 4)}
        for i, j in farthest_first(4, 4)
    ]
    second = [
        {"orb": x * 16 + lax.rem(z + i, 8) * 2 + lax.rem(core + j, 2), "wall": place}
        for i, j in farthest_first(8, 2)
    ]
    return first, second


def send(source, target, send_sem, recv_sem, device):
    return pltpu.make_async_remote_copy(
        src_ref=source,
        dst_ref=target,
        send_sem=send_sem,
        recv_sem=recv_sem,
        device_id=device,
        device_id_type=MESH,
    )


def step_kernel(
    pair_in, wpair_in, ghost_in, count_in, own_in, wall_in, rate_out, accel_out, step_ref,
    pair_ref, wpair_ref, ghost_ref, count_ref, own_ref, wall_ref, rate_ref, accel_ref,
    blocks, outgoing, arrived, edges, edges_in, held, slots,
    sf, sh, sc, wf, wc, tf, sums, wsums,
    near0, near1, wall0, wall1, own_rows,
    send_sems, recv_sems, peak_send, peak_recv, load_sems, store_sems,
):
    orb = lax.axis_index("orb")
    place = lax.axis_index("wall")
    places = lax.axis_size("wall")
    partners = [{"orb": flipped(orb, q)} for q in range(1, 8)]
    above = {"wall": lax.rem(place + 1, places)}
    below = {"wall": lax.rem(place + places - 1, places)}
    phases = rounds()

    sources = pair_in, wpair_in, ghost_in, count_in, own_in, wall_in
    targets = pair_ref, wpair_ref, ghost_ref, count_ref, own_ref, wall_ref
    loads = [
        pltpu.make_async_copy(source, target, load_sems.at[n])
        for n, (source, target) in enumerate(zip(sources, targets))
    ]
    for copy in loads:
        copy.start()
    barrier = pltpu.get_barrier_semaphore()
    greeted = [device for pair in zip(*phases) for device in pair] + [*partners, above, below]
    for device in greeted:
        pl.semaphore_signal(barrier, inc=1, device_id=device, device_id_type=MESH)

    for copy in loads:
        copy.wait()
    for b in range(NB):
        blocks[b] = own_ref[:, LN * b : LN * b + LN]
    for q in range(7):
        for g in range(GH):
            outgoing[q, 8 * g : 8 * g + 8, :] = blocks[ghost_ref[q, g]]
    lane_row = lax.broadcasted_iota(jnp.int32, (1, LN), 1)

    def live_block(b):
        block = wall_ref[:, LN * b : LN * b + LN]
        return stack([block[:3], jnp.where(lane_row < count_ref[b], block[3:4], 0.0)])

    edges[0] = live_block(0)
    edges[1] = live_block(WB - 1)

    row = lax.broadcasted_iota(jnp.int32, (LN, 2 * LN), 0)
    lane = lax.broadcasted_iota(jnp.int32, (LN, 2 * LN), 1)
    doubled = jnp.where(row == lane // 32 * 16 + lane % 16, 1.0, 0.0).astype(BF16)

    def keep_sources(first, group):
        columns = []
        for n, block in enumerate(group):
            geometry, column = source_tiles(block)
            sf[first + n] = geometry.astype(BF16).T
            sh[first + n] = jnp.broadcast_to(half_scale * block[6:7], (LN, LN)).T
            columns.append(column)
        wide_columns = product(stack(columns), doubled).astype(BF16)
        for n in range(len(group)):
            sc[first + n] = wide_columns[32 * n : 32 * n + 32]

    def build_own(t, carry):
        keep_sources(t * GH, [blocks[t * GH + n] for n in range(GH)])
        return carry

    def keep_wall(b, block):
        geometry, columns = wall_tiles(block)
        wf[b] = geometry.astype(BF16).T
        wc[b] = product(columns, doubled).astype(BF16)

    def build_target(b, carry):
        tf[b] = jnp.concatenate([t.astype(BF16) for t in target_tiles(blocks[b])], axis=1)
        return carry

    def diagonal(tile):
        zero = jnp.zeros_like(tile)
        return stack([jnp.concatenate([tile, zero], axis=1), jnp.concatenate([zero, tile], axis=1)])

    lax.fori_loop(0, NB, build_target, 0, unroll=2)
    lax.fori_loop(0, NB // GH, build_own, 0)
    for b in range(WB):
        keep_wall(b + 1, live_block(b))

    pl.semaphore_wait(barrier, len(greeted))
    edge_copies = [
        send(edges.at[n], edges_in.at[n], send_sems.at[7 + n], recv_sems.at[7 + n], device)
        for n, device in enumerate((below, above))
    ]
    ghost_copies = [
        send(outgoing.at[q], arrived.at[q], send_sems.at[q], recv_sems.at[q], partners[q])
        for q in range(7)
    ]
    for copy in edge_copies:
        copy.start()
    for q in (6, 5, 3, 4, 2, 1, 0):
        ghost_copies[q].start()

    for copy in edge_copies:
        copy.wait()
    keep_wall(0, jnp.where(place > 0, edges_in[1], 0.0))
    keep_wall(NW - 1, jnp.where(place < places - 1, edges_in[0], 0.0))

    def gathered(ref, indices):
        return stack([ref[j] for j in indices])

    def paired(ref, indices):
        return jnp.concatenate([gathered(ref, indices[0::2]), gathered(ref, indices[1::2])], axis=1)

    def matrix(cubed, pull):
        terms = two_terms(cubed), two_terms(pull)
        rows = []
        for top in range(0, LN, 16):
            for part in range(2):
                rows.append(jnp.concatenate([t[part][top : top + 16] for t in terms], axis=1))
        return stack(rows)

    group = 4
    tall = KW // 2 * LN

    def wall_geometry(t, wall):
        for n in range(group):
            b = t * group + n
            tiles = paired(wf, [wpair_ref[k, b] for k in range(KW)])
            wall[n * tall : (n + 1) * tall] = product(tiles, diagonal(tf[b, :, :LN]))

    def wall_forces(t, wall, at):
        past = []
        for n in range(group):
            b = t * group + n
            total = jnp.zeros((16, 2 * LN), F32)
            for k in range(KW):
                if len(past) >= WALL_LAG:
                    row = pl.multiple_of(group * tall + 16 * at, 16)
                    wall[pl.ds(row, 16), :] = past[len(past) - WALL_LAG]
                half, side = pl.ds(n * tall + k // 2 * LN, LN), k % 2 * LN
                s, cubed = falloff_of(jnp.maximum(wall[half, side : side + LN], 1e-30))
                total += product(wc[wpair_ref[k, b]], matrix(cubed, cubed * s))
                past.append(total)
            wsums[b] = total[:8] + total[8:]

    wall_geometry(0, wall0)

    def two_walls(t, carry):
        wall_geometry(2 * t + 1, wall1)
        at = lax.div(t, NB)
        wall_forces(2 * t, wall0, at)
        wall_geometry(jnp.minimum(2 * t + 2, NB // group - 1), wall0)
        wall_forces(2 * t + 1, wall1, at)
        return carry

    lax.fori_loop(0, NB // group // 2, two_walls, 0)

    for q in (0, 1, 2, 4, 3, 5, 6):
        ghost_copies[q].wait()
        keep_sources(NB + q * GH, [arrived[q, 8 * g : 8 * g + 8, :] for g in range(GH)])

    def geometry(b, near):
        for n in range(0, K, GROUP):
            indices = [pair_ref[k, b] for k in range(n, n + GROUP)]
            near[pl.ds(n * LN, GROUP * LN), :] = product(gathered(sf, indices), tf[b])

    def forces(b, near):
        total = jnp.zeros((32, 2 * LN), F32)
        half = half_scale * blocks[b, 6:7, :]
        for k in range(K):
            j, tile = pair_ref[k, b], pl.ds(k * LN, LN)
            dist_sq = jnp.maximum(near[tile, :LN], 1e-30)
            s, cubed = falloff_of(dist_sq)
            damp = (dist_sq + eps_scaled) * (sh[j] + half)
            drag = jnp.minimum(near[tile, LN:], 0.0) / damp
            total += product(sc[j], matrix(cubed, cubed * (drag - s)))
        sums[b] = total[:16] + total[16:]

    geometry(0, near0)
    stages = near0, near1

    def some_blocks(t, carry):
        for n in range(UNROLL):
            b = UNROLL * t + n
            geometry(jnp.minimum(b + 1, NB - 1), stages[(n + 1) % 2])
            forces(b, stages[n % 2])
        return carry

    lax.fori_loop(0, NB // UNROLL, some_blocks, 0)

    for b in range(NB):
        own_rows[8 * b : 8 * b + 8, :] = blocks[b]
    state = [own_rows[pl.ds(r, NB, stride=8), :] for r in range(8)]
    y = [(r - center) * inv_support for r in state[:3]]
    v, rho = state[3:6], state[6]
    push = pressure_of(rho) / (rho * rho)
    weigh = [sums[:, r, :LN] for r in range(16)]
    pull = [sums[:, r, LN:] for r in range(16)]
    wweigh = [wsums[:, r, :LN] for r in range(4)]
    wpull = [wsums[:, r, LN:] for r in range(4)]
    square = jnp.zeros((NB, LN), F32)
    forces_out = []
    for c in range(3):
        near = y[c] * weigh[7] - weigh[c]
        wnear = y[c] * wweigh[3] - wweigh[c]
        pressed = push * (near + 2.0 * wnear) + y[c] * weigh[15] - weigh[8 + c]
        pulled = 3.0 * cohesion * near + pull_scale * (y[c] * pull[7] - pull[c])
        pulled += 3.0 * adhesion * wnear - wall_pull_scale * (y[c] * wpull[3] - wpull[c])
        force = (-grad_coeff * support) * pressed - support * pulled
        if c == 2:
            force = force - gravity
        square += force * force
        forces_out.append(force)
    best = jnp.max(jnp.max(square, axis=0, keepdims=True), axis=1, keepdims=True)
    held[0] = jnp.broadcast_to(jnp.sqrt(best), (1, LN))

    def phase_copies(n):
        return [
            send(held.at[n], slots.at[n, t], peak_send.at[n, t], peak_recv.at[n, t], device)
            for t, device in enumerate(phases[n])
        ]

    copies = phase_copies(0)
    for copy in copies:
        copy.start()
    rate = (
        dot3(v, y) * (weigh[7] + wweigh[3])
        - dot3(v, [weigh[c] + wweigh[c] for c in range(3)])
        - dot3(weigh[3:6], y)
        + weigh[6]
    )
    rate_ref[...] = (grad_coeff * support) * rate
    for c in range(3):
        for b in range(NB):
            accel_ref[c : c + 1, LN * b : LN * b + LN] = forces_out[c][b : b + 1]
    stores = [
        pltpu.make_async_copy(rate_ref, rate_out, store_sems.at[0]),
        pltpu.make_async_copy(accel_ref, accel_out, store_sems.at[1]),
    ]
    for copy in stores:
        copy.start()
    for n in range(2):
        best = held[n]
        for t, copy in reversed(list(enumerate(copies))):
            copy.wait()
            best = jnp.maximum(best, slots[n, t])
        held[n + 1] = best
        if n == 0:
            copies = phase_copies(1)
            for copy in copies:
                copy.start()
    step_ref[0, 0] = jnp.max(courant * jnp.sqrt(smoothing / (best + 1e-06)))
    for copy in stores:
        copy.wait()


def handed_on(rates, acceleration):
    def kernel(rate_ref, accel_ref, rate_out, accel_out):
        rate_out[...] = rate_ref[...]
        accel_out[...] = accel_ref[...]

    vmem = pl.BlockSpec(memory_space=pltpu.VMEM)
    shapes = jax.ShapeDtypeStruct((NB, LN), F32), jax.ShapeDtypeStruct((3, NB * LN), F32)
    return pl.pallas_call(
        kernel, name="handed_on", out_shape=shapes, in_specs=[vmem, vmem], out_specs=(vmem, vmem)
    )(rates, acceleration)


def per_device(fluid_state, ghost_list, pair_list, wall_state, wall_count, wall_pairs):
    anywhere = pl.BlockSpec(memory_space=pl.ANY)
    smem = pl.BlockSpec(memory_space=pltpu.SMEM)
    rates, acceleration, step = pl.pallas_call(
        step_kernel,
        name="step",
        out_shape=(
            jax.ShapeDtypeStruct((NB, LN), F32),
            jax.ShapeDtypeStruct((3, NB * LN), F32),
            jax.ShapeDtypeStruct((1, 1), F32),
        ),
        in_specs=[anywhere] * 6,
        out_specs=(anywhere, anywhere, smem),
        scratch_shapes=[
            pltpu.SMEM((K, NB), jnp.int32),
            pltpu.SMEM((KW, NB), jnp.int32),
            pltpu.SMEM((7, GH), jnp.int32),
            pltpu.SMEM((WB,), jnp.int32),
            pltpu.VMEM((8, NB * LN), F32),
            pltpu.VMEM((4, WB * LN), F32),
            pltpu.VMEM((NB, LN), F32),
            pltpu.VMEM((3, NB * LN), F32),
            pltpu.VMEM((NB, 8, LN), F32),
            pltpu.VMEM((7, GH * 8, LN), F32),
            pltpu.VMEM((7, GH * 8, LN), F32),
            pltpu.VMEM((2, 4, LN), F32),
            pltpu.VMEM((2, 4, LN), F32),
            pltpu.VMEM((3, 1, LN), F32),
            pltpu.VMEM((2, 15, 1, LN), F32),
            pltpu.VMEM((NC, LN, LN), BF16),
            pltpu.VMEM((NC, LN, LN), F32),
            pltpu.VMEM((NC, 32, 2 * LN), BF16),
            pltpu.VMEM((NW, LN, LN), BF16),
            pltpu.VMEM((NW, 16, 2 * LN), BF16),
            pltpu.VMEM((NB, LN, 2 * LN), BF16),
            pltpu.VMEM((NB, 16, 2 * LN), F32),
            pltpu.VMEM((NB, 8, 2 * LN), F32),
        ]
        + [pltpu.VMEM((K * LN, 2 * LN), F32)] * 2
        + [pltpu.VMEM((4 * KW // 2 * LN + 32, 2 * LN), F32)] * 2
        + [
            pltpu.VMEM((NB * 8, LN), F32),
            pltpu.SemaphoreType.DMA((9,)),
            pltpu.SemaphoreType.DMA((9,)),
            pltpu.SemaphoreType.DMA((2, 15)),
            pltpu.SemaphoreType.DMA((2, 15)),
            pltpu.SemaphoreType.DMA((6,)),
            pltpu.SemaphoreType.DMA((2,)),
        ],
        compiler_params=pltpu.CompilerParams(collective_id=0, has_side_effects=True),
    )(pair_list.T, wall_pairs.T, ghost_list, wall_count, fluid_state, wall_state)
    rates, acceleration = handed_on(rates, acceleration)
    return (rates.reshape(-1), acceleration, step.reshape(()))


def solution(mesh):
    return jax.shard_map(
        per_device,
        mesh=mesh,
        in_specs=(
            P(None, ("orb", "wall")),
            P(None, ("orb", "wall")),
            P(("orb", "wall"), None),
            P(None, ("orb", "wall")),
            P(("orb", "wall")),
            P(("orb", "wall"), None),
        ),
        out_specs=(P(("orb", "wall")), P(None, ("orb", "wall")), P()),
        check_vma=False,
    )
```

```python
import jax
import jax.numpy as jnp
from jax import lax
from jax.experimental import pallas as pl
from jax.experimental.pallas import tpu as pltpu
from jax.sharding import PartitionSpec as P

NB = 24
K = 14
KW = 4
GH = 6
WB = 6
EB = 1
NC = NB + 7 * GH
NW = WB + 2 * EB
LN = 128
UNROLL = 4
WALL_LAG = 12
GROUP = 2

smoothing = 0.1
support = 0.3
kernel_norm = 21.0 / (2.0 * 3.141592653589793 * support**3)
grad_coeff = -20.0 / support**2 * kernel_norm
tait_coeff = 25.0 / 7.0
visc_coeff = 0.05
cohesion = 2000.0
adhesion = 2000.0
gravity = 9.81
courant = 0.25

center = 0.3
inv_support = 1.0 / support
eps_scaled = 0.0001 / support**2
pull_scale = 4.0 * cohesion
wall_pull_scale = 4.0 * adhesion
visc_scaled = visc_coeff * -grad_coeff / support / pull_scale
half_scale = 0.5 / visc_scaled

F32 = jnp.float32
BF16 = jnp.bfloat16


def split(value):
    parts = []
    for _ in range(2):
        high = value.astype(BF16).astype(F32)
        parts.append(high)
        value = value - high
    parts.append(value.astype(BF16).astype(F32))
    return parts


def two_terms(value):
    high = value.astype(BF16)
    return high, (value - high.astype(F32)).astype(BF16)


def pressure_of(density):
    return tait_coeff * (density**7 - 1.0)


def dot3(a, b):
    return a[0] * b[0] + a[1] * b[1] + a[2] * b[2]


def rows_of(block):
    return [block[c : c + 1] for c in range(block.shape[0])]


def stack(rows):
    return jnp.concatenate(rows, axis=0)


CROSS = ((0, 0), (0, 1), (0, 2), (1, 0), (1, 1), (2, 0))


def scaled_rows(block):
    rows = rows_of(block)
    y = [(row - center) * inv_support for row in rows[:3]]
    return y, rows[3:6], rows[6], rows[7]


def wide(groups):
    rows = stack(groups)
    spare = LN - rows.shape[0]
    return stack([rows, jnp.zeros((spare, LN), F32)]) if spare else rows


def source_tiles(block):
    y, v, rho, mass = scaled_rows(block)
    half = half_scale * rho
    one, zero = jnp.ones_like(mass), jnp.zeros_like(mass)
    norm, flow = dot3(y, y), dot3(v, y)
    terms = split(stack(y + v + [half, zero]))
    sums = split(stack([norm, flow, one, one, one, zero, zero, zero]))
    push = pressure_of(rho) / (rho * rho)
    heavy = stack(y + v + [flow, one]) * mass
    pushed = heavy * push
    hh, hl = two_terms(heavy)
    ph, pl_ = two_terms(pushed)
    return wide([terms[j] for j, _ in CROSS] + sums), stack([hh, ph, hl, pl_])


def wall_tiles(block):
    rows = rows_of(block)
    y = [(row - center) * inv_support for row in rows[:3]]
    mass = rows[3]
    one, zero = jnp.ones_like(mass), jnp.zeros_like(mass)
    terms = split(stack(y + [zero] * 5))
    sums = split(stack([dot3(y, y), zero, one, one, one, zero, zero, zero]))
    heavy = stack(y + [one, zero, zero, zero, zero]) * mass
    hh, hl = two_terms(heavy)
    return wide([terms[j] for j, _ in CROSS] + sums), stack([hh, hl])


def target_tiles(block):
    y, v, _, mass = scaled_rows(block)
    one, zero = jnp.ones_like(mass), jnp.zeros_like(mass)
    norm, flow = dot3(y, y), dot3(v, y)
    far = split(stack([-2.0 * c for c in y] + [zero] * 5))
    near = split(stack([-c for c in v] + [-c for c in y] + [zero] * 2))
    far_sum = stack([one, zero] + split(norm) + [zero] * 3)
    near_sum = stack([zero, one] + split(flow) + [zero] * 3)
    return (
        wide([far[i] for _, i in CROSS] + [far_sum] * 3),
        wide([near[i] for _, i in CROSS] + [near_sum] * 3),
    )


def falloff_of(dist_sq):
    s = jnp.maximum(1.0 - dist_sq * lax.rsqrt(dist_sq), 0.0)
    return s, s * s * s


def product(left, right):
    return jnp.dot(left, right, preferred_element_type=F32)


MESH = pl.DeviceIdType.MESH


def flipped(place, pattern):
    partner = place
    for bit in (1, 2, 4):
        if pattern & bit:
            partner = partner + bit - 2 * bit * lax.rem(lax.div(place, bit), 2)
    return partner


def farthest_first(long, short):
    steps = [(i, j) for i in range(long) for j in range(short) if i or j]
    return sorted(steps, key=lambda step: -min(step[0], long - step[0]) - min(step[1], short - step[1]))


def rounds():
    orb = lax.axis_index("orb")
    place = lax.axis_index("wall")
    x, rest = lax.div(orb, 16), lax.rem(orb, 16)
    z, core = lax.div(rest, 2), lax.rem(rest, 2)
    first = [
        {"orb": lax.rem(x + i, 4) * 16 + rest, "wall": lax.rem(place + j, 4)}
        for i, j in farthest_first(4, 4)
    ]
    second = [
        {"orb": x * 16 + lax.rem(z + i, 8) * 2 + lax.rem(core + j, 2), "wall": place}
        for i, j in farthest_first(8, 2)
    ]
    return first, second


def send(source, target, send_sem, recv_sem, device):
    return pltpu.make_async_remote_copy(
        src_ref=source,
        dst_ref=target,
        send_sem=send_sem,
        recv_sem=recv_sem,
        device_id=device,
        device_id_type=MESH,
    )


def step_kernel(
    pair_in, wpair_in, ghost_in, count_in, own_in, wall_in, rate_out, accel_out, step_ref,
    pair_ref, wpair_ref, ghost_ref, count_ref, own_ref, wall_ref, rate_ref, accel_ref,
    blocks, outgoing, arrived, edges, edges_in, held, slots,
    sf, sh, sc, wf, wc, tf, sums, wsums,
    near0, near1, wall0, wall1, own_rows,
    send_sems, recv_sems, peak_send, peak_recv, load_sems, store_sems,
):
    orb = lax.axis_index("orb")
    place = lax.axis_index("wall")
    places = lax.axis_size("wall")
    partners = [{"orb": flipped(orb, q)} for q in range(1, 8)]
    above = {"wall": lax.rem(place + 1, places)}
    below = {"wall": lax.rem(place + places - 1, places)}
    phases = rounds()

    sources = pair_in, wpair_in, ghost_in, count_in, own_in, wall_in
    targets = pair_ref, wpair_ref, ghost_ref, count_ref, own_ref, wall_ref
    loads = [
        pltpu.make_async_copy(source, target, load_sems.at[n])
        for n, (source, target) in enumerate(zip(sources, targets))
    ]
    for copy in loads:
        copy.start()
    barrier = pltpu.get_barrier_semaphore()
    greeted = [device for pair in zip(*phases) for device in pair] + [*partners, above, below]
    for device in greeted:
        pl.semaphore_signal(barrier, inc=1, device_id=device, device_id_type=MESH)

    for copy in loads:
        copy.wait()
    for b in range(NB):
        blocks[b] = own_ref[:, LN * b : LN * b + LN]
    for q in range(7):
        for g in range(GH):
            outgoing[q, 8 * g : 8 * g + 8, :] = blocks[ghost_ref[q, g]]
    lane_row = lax.broadcasted_iota(jnp.int32, (1, LN), 1)

    def live_block(b):
        block = wall_ref[:, LN * b : LN * b + LN]
        return stack([block[:3], jnp.where(lane_row < count_ref[b], block[3:4], 0.0)])

    edges[0] = live_block(0)
    edges[1] = live_block(WB - 1)

    row = lax.broadcasted_iota(jnp.int32, (LN, 2 * LN), 0)
    lane = lax.broadcasted_iota(jnp.int32, (LN, 2 * LN), 1)
    doubled = jnp.where(row == lane // 32 * 16 + lane % 16, 1.0, 0.0).astype(BF16)

    def keep_sources(first, group):
        columns = []
        for n, block in enumerate(group):
            geometry, column = source_tiles(block)
            sf[first + n] = geometry.astype(BF16).T
            sh[first + n] = jnp.broadcast_to(half_scale * block[6:7], (LN, LN)).T
            columns.append(column)
        wide_columns = product(stack(columns), doubled).astype(BF16)
        for n in range(len(group)):
            sc[first + n] = wide_columns[32 * n : 32 * n + 32]

    def build_own(t, carry):
        keep_sources(t * GH, [blocks[t * GH + n] for n in range(GH)])
        return carry

    def keep_wall(b, block):
        geometry, columns = wall_tiles(block)
        wf[b] = geometry.astype(BF16).T
        wc[b] = product(columns, doubled).astype(BF16)

    def build_target(b, carry):
        tf[b] = jnp.concatenate([t.astype(BF16) for t in target_tiles(blocks[b])], axis=1)
        return carry

    def diagonal(tile):
        zero = jnp.zeros_like(tile)
        return stack([jnp.concatenate([tile, zero], axis=1), jnp.concatenate([zero, tile], axis=1)])

    lax.fori_loop(0, NB, build_target, 0, unroll=6)
    lax.fori_loop(0, NB // GH, build_own, 0)
    for b in range(WB):
        keep_wall(b + 1, live_block(b))

    pl.semaphore_wait(barrier, len(greeted))
    edge_copies = [
        send(edges.at[n], edges_in.at[n], send_sems.at[7 + n], recv_sems.at[7 + n], device)
        for n, device in enumerate((below, above))
    ]
    ghost_copies = [
        send(outgoing.at[q], arrived.at[q], send_sems.at[q], recv_sems.at[q], partners[q])
        for q in range(7)
    ]
    for copy in edge_copies:
        copy.start()
    for q in (6, 5, 3, 4, 2, 1, 0):
        ghost_copies[q].start()

    for copy in edge_copies:
        copy.wait()
    keep_wall(0, jnp.where(place > 0, edges_in[1], 0.0))
    keep_wall(NW - 1, jnp.where(place < places - 1, edges_in[0], 0.0))

    def gathered(ref, indices):
        return stack([ref[j] for j in indices])

    def paired(ref, indices):
        return jnp.concatenate([gathered(ref, indices[0::2]), gathered(ref, indices[1::2])], axis=1)

    def matrix(cubed, pull):
        terms = two_terms(cubed), two_terms(pull)
        rows = []
        for top in range(0, LN, 16):
            for part in range(2):
                rows.append(jnp.concatenate([t[part][top : top + 16] for t in terms], axis=1))
        return stack(rows)

    group = 4
    tall = KW // 2 * LN

    def wall_geometry(t, wall):
        for n in range(group):
            b = t * group + n
            tiles = paired(wf, [wpair_ref[k, b] for k in range(KW)])
            wall[n * tall : (n + 1) * tall] = product(tiles, diagonal(tf[b, :, :LN]))

    def wall_forces(t, wall, at):
        past = []
        for n in range(group):
            b = t * group + n
            total = jnp.zeros((16, 2 * LN), F32)
            for k in range(KW):
                if len(past) >= WALL_LAG:
                    row = pl.multiple_of(group * tall + 16 * at, 16)
                    wall[pl.ds(row, 16), :] = past[len(past) - WALL_LAG]
                half, side = pl.ds(n * tall + k // 2 * LN, LN), k % 2 * LN
                s, cubed = falloff_of(jnp.maximum(wall[half, side : side + LN], 1e-30))
                total += product(wc[wpair_ref[k, b]], matrix(cubed, cubed * s))
                past.append(total)
            wsums[b] = total[:8] + total[8:]

    wall_geometry(0, wall0)

    def two_walls(t, carry):
        wall_geometry(2 * t + 1, wall1)
        at = lax.div(t, NB)
        wall_forces(2 * t, wall0, at)
        wall_geometry(jnp.minimum(2 * t + 2, NB // group - 1), wall0)
        wall_forces(2 * t + 1, wall1, at)
        return carry

    lax.fori_loop(0, NB // group // 2, two_walls, 0)

    for q in (0, 1, 2, 4, 3, 5, 6):
        ghost_copies[q].wait()
        keep_sources(NB + q * GH, [arrived[q, 8 * g : 8 * g + 8, :] for g in range(GH)])

    def geometry(b, near):
        for n in range(0, K, GROUP):
            indices = [pair_ref[k, b] for k in range(n, n + GROUP)]
            near[pl.ds(n * LN, GROUP * LN), :] = product(gathered(sf, indices), tf[b])

    def forces(b, near):
        total = jnp.zeros((32, 2 * LN), F32)
        half = half_scale * blocks[b, 6:7, :]
        for k in range(K):
            j, tile = pair_ref[k, b], pl.ds(k * LN, LN)
            dist_sq = jnp.maximum(near[tile, :LN], 1e-30)
            s, cubed = falloff_of(dist_sq)
            damp = (dist_sq + eps_scaled) * (sh[j] + half)
            drag = jnp.minimum(near[tile, LN:], 0.0) / damp
            total += product(sc[j], matrix(cubed, cubed * (drag - s)))
        sums[b] = total[:16] + total[16:]

    geometry(0, near0)
    stages = near0, near1

    def some_blocks(t, carry):
        for n in range(UNROLL):
            b = UNROLL * t + n
            geometry(jnp.minimum(b + 1, NB - 1), stages[(n + 1) % 2])
            forces(b, stages[n % 2])
        return carry

    lax.fori_loop(0, NB // UNROLL, some_blocks, 0)

    for b in range(NB):
        own_rows[8 * b : 8 * b + 8, :] = blocks[b]
    state = [own_rows[pl.ds(r, NB, stride=8), :] for r in range(8)]
    y = [(r - center) * inv_support for r in state[:3]]
    v, rho = state[3:6], state[6]
    push = pressure_of(rho) / (rho * rho)
    weigh = [sums[:, r, :LN] for r in range(16)]
    pull = [sums[:, r, LN:] for r in range(16)]
    wweigh = [wsums[:, r, :LN] for r in range(4)]
    wpull = [wsums[:, r, LN:] for r in range(4)]
    square = jnp.zeros((NB, LN), F32)
    forces_out = []
    for c in range(3):
        near = y[c] * weigh[7] - weigh[c]
        wnear = y[c] * wweigh[3] - wweigh[c]
        pressed = push * (near + 2.0 * wnear) + y[c] * weigh[15] - weigh[8 + c]
        pulled = 3.0 * cohesion * near + pull_scale * (y[c] * pull[7] - pull[c])
        pulled += 3.0 * adhesion * wnear - wall_pull_scale * (y[c] * wpull[3] - wpull[c])
        force = (-grad_coeff * support) * pressed - support * pulled
        if c == 2:
            force = force - gravity
        square += force * force
        forces_out.append(force)
    best = jnp.max(jnp.max(square, axis=0, keepdims=True), axis=1, keepdims=True)
    held[0] = jnp.broadcast_to(jnp.sqrt(best), (1, LN))

    def phase_copies(n):
        return [
            send(held.at[n], slots.at[n, t], peak_send.at[n, t], peak_recv.at[n, t], device)
            for t, device in enumerate(phases[n])
        ]

    copies = phase_copies(0)
    for copy in copies:
        copy.start()
    rate = (
        dot3(v, y) * (weigh[7] + wweigh[3])
        - dot3(v, [weigh[c] + wweigh[c] for c in range(3)])
        - dot3(weigh[3:6], y)
        + weigh[6]
    )
    rate_ref[...] = (grad_coeff * support) * rate
    for c in range(3):
        for b in range(NB):
            accel_ref[c : c + 1, LN * b : LN * b + LN] = forces_out[c][b : b + 1]
    stores = [
        pltpu.make_async_copy(rate_ref, rate_out, store_sems.at[0]),
        pltpu.make_async_copy(accel_ref, accel_out, store_sems.at[1]),
    ]
    for copy in stores:
        copy.start()
    for n in range(2):
        best = held[n]
        for t, copy in reversed(list(enumerate(copies))):
            copy.wait()
            best = jnp.maximum(best, slots[n, t])
        held[n + 1] = best
        if n == 0:
            copies = phase_copies(1)
            for copy in copies:
                copy.start()
    step_ref[0, 0] = jnp.max(courant * jnp.sqrt(smoothing / (best + 1e-06)))
    for copy in stores:
        copy.wait()


def handed_on(rates, acceleration):
    def kernel(rate_ref, accel_ref, rate_out, accel_out):
        rate_out[...] = rate_ref[...]
        accel_out[...] = accel_ref[...]

    vmem = pl.BlockSpec(memory_space=pltpu.VMEM)
    shapes = jax.ShapeDtypeStruct((NB, LN), F32), jax.ShapeDtypeStruct((3, NB * LN), F32)
    return pl.pallas_call(
        kernel, name="handed_on", out_shape=shapes, in_specs=[vmem, vmem], out_specs=(vmem, vmem)
    )(rates, acceleration)


def per_device(fluid_state, ghost_list, pair_list, wall_state, wall_count, wall_pairs):
    anywhere = pl.BlockSpec(memory_space=pl.ANY)
    smem = pl.BlockSpec(memory_space=pltpu.SMEM)
    rates, acceleration, step = pl.pallas_call(
        step_kernel,
        name="step",
        out_shape=(
            jax.ShapeDtypeStruct((NB, LN), F32),
            jax.ShapeDtypeStruct((3, NB * LN), F32),
            jax.ShapeDtypeStruct((1, 1), F32),
        ),
        in_specs=[anywhere] * 6,
        out_specs=(anywhere, anywhere, smem),
        scratch_shapes=[
            pltpu.SMEM((K, NB), jnp.int32),
            pltpu.SMEM((KW, NB), jnp.int32),
            pltpu.SMEM((7, GH), jnp.int32),
            pltpu.SMEM((WB,), jnp.int32),
            pltpu.VMEM((8, NB * LN), F32),
            pltpu.VMEM((4, WB * LN), F32),
            pltpu.VMEM((NB, LN), F32),
            pltpu.VMEM((3, NB * LN), F32),
            pltpu.VMEM((NB, 8, LN), F32),
            pltpu.VMEM((7, GH * 8, LN), F32),
            pltpu.VMEM((7, GH * 8, LN), F32),
            pltpu.VMEM((2, 4, LN), F32),
            pltpu.VMEM((2, 4, LN), F32),
            pltpu.VMEM((3, 1, LN), F32),
            pltpu.VMEM((2, 15, 1, LN), F32),
            pltpu.VMEM((NC, LN, LN), BF16),
            pltpu.VMEM((NC, LN, LN), F32),
            pltpu.VMEM((NC, 32, 2 * LN), BF16),
            pltpu.VMEM((NW, LN, LN), BF16),
            pltpu.VMEM((NW, 16, 2 * LN), BF16),
            pltpu.VMEM((NB, LN, 2 * LN), BF16),
            pltpu.VMEM((NB, 16, 2 * LN), F32),
            pltpu.VMEM((NB, 8, 2 * LN), F32),
        ]
        + [pltpu.VMEM((K * LN, 2 * LN), F32)] * 2
        + [pltpu.VMEM((4 * KW // 2 * LN + 32, 2 * LN), F32)] * 2
        + [
            pltpu.VMEM((NB * 8, LN), F32),
            pltpu.SemaphoreType.DMA((9,)),
            pltpu.SemaphoreType.DMA((9,)),
            pltpu.SemaphoreType.DMA((2, 15)),
            pltpu.SemaphoreType.DMA((2, 15)),
            pltpu.SemaphoreType.DMA((6,)),
            pltpu.SemaphoreType.DMA((2,)),
        ],
        compiler_params=pltpu.CompilerParams(collective_id=0, has_side_effects=True),
    )(pair_list.T, wall_pairs.T, ghost_list, wall_count, fluid_state, wall_state)
    rates, acceleration = handed_on(rates, acceleration)
    return (rates.reshape(-1), acceleration, step.reshape(()))


def solution(mesh):
    return jax.shard_map(
        per_device,
        mesh=mesh,
        in_specs=(
            P(None, ("orb", "wall")),
            P(None, ("orb", "wall")),
            P(("orb", "wall"), None),
            P(None, ("orb", "wall")),
            P(("orb", "wall")),
            P(("orb", "wall"), None),
        ),
        out_specs=(P(("orb", "wall")), P(None, ("orb", "wall")), P()),
        check_vma=False,
    )
```
